128 devices in a mesh: span: 16 (over z, y_hi, core), group: 8 (over y_lo, x).
Axes of the slice: x: 4, y: 4 (y_hi: 2, y_lo: 2; y = y_hi * 2 + y_lo), z: 4, core: 2. Of those that a mesh axis runs over, the one named last changes fastest.
Arguments:
- air_temp: float32 [8, 256, 8192], P('group', 'span'), may hold values from -6 to 6
- air_vel: float32 [8, 256, 8192], P('group', 'span'), may hold values from -0.3 to 0.3
- air_kappa: float32 [8, 256, 8192], P('group', 'span'), may hold values from 0.02 to 0.2
- group_width: int32 [8], P('group'), may hold values from 2048 to 8192
- sub_temp: float32 [16384, 64], P(('span', 'group')), may hold values from -6 to 6
- sub_coupling: bfloat16 [16384, 4, 4096], P(('span', 'group')), may hold values from -0.1875 to 0.1875
- neighbors: int32 [16384, 4], P(('span', 'group')), may hold values from 0 to 16383, as said below
- iface_count: int32 [128], P(('span', 'group')), may hold values from 768 to 1024
- iface_seg: int32 [131072], P(('span', 'group')), may hold values from 0 to 2047, as said below
- iface_owner: int32 [131072, 1], P(('span', 'group')), may hold values from 0 to 127; in each aligned block of 1024 rows (0 to 1023, 1024 to 2047, ...) at most 16 rows name the same one
- iface_block: int32 [131072], P(('span', 'group')), may hold values from 0 to 127
Outputs:
- air_out: float32 [8, 256, 8192], P('group', 'span')
- sub_out: float32 [16384, 64], P(('span', 'group'))
The draws below stay inside these ranges and needn't reach their ends.
Inputs may be any that keep to these rules, and one draw needn't show every extreme that they name: `neighbors`: the first coupled block of every block is itself; the others lie on the same device or the one just before or after it along span+group (no wrap). `iface_seg`: the segments of one device's rows are all different. `iface_owner`: among the rows of one device no owner is named more than 16 times. `iface_count`: the live rows of a device are its first ones.
All inputs are finite; a program needn't handle non-finite values.
Results may differ from the reference program's by a relative error of at most 0.0016.
Values may be sent and summed in bfloat16 or wider, within the bound.
A program may use at most 64 MiB of HBM per device.

```python
import math
import jax
import jax.numpy as jnp
import numpy as np
from jax import lax

CA = 16
PW = 8192
STEPS = 4
SSTEPS = 2
NODES = 64
NNB = 4
BDEV = 128
IROWS = 1024
G = 8
NL = 256
NBLK = 16384
NSEG = 2048
CAP = 16
DEVICES = 128


def draw_iface_seg(key, part):

    def one(k):
        first, second = jax.random.split(k)
        rest = jax.random.permutation(first, NSEG - 1)[:IROWS - 1].astype(jnp.int32)
        full = jnp.concatenate([jnp.full((1,), NSEG - 1, jnp.int32), rest])
        return full[jax.random.permutation(second, IROWS)]
    keys = jax.random.split(jax.random.fold_in(key, 11), DEVICES)
    return jax.vmap(one)(keys).reshape(-1).astype(jnp.int32)


def draw_neighbors(key, part):
    first, second = jax.random.split(jax.random.fold_in(key, 23))
    owner = jnp.arange(NBLK, dtype=jnp.int32) // BDEV
    offset = jax.random.randint(first, (NBLK, NNB - 1), -1, 2, dtype=jnp.int32)
    other = jnp.clip(owner[:, None] + offset, 0, DEVICES - 1)
    local = jax.random.randint(second, (NBLK, NNB - 1), 0, BDEV, dtype=jnp.int32)
    itself = jnp.arange(NBLK, dtype=jnp.int32)[:, None]
    return jnp.concatenate([itself, other * BDEV + local], axis=1).astype(jnp.int32)


def set_ends(entries, key, low, largest):
    extent = entries.shape
    spot = [jax.random.randint(jax.random.fold_in(key, axis), (), 0, extent[axis]) for axis in range(len(extent))]
    entries = entries.at[tuple(spot)].set(low)
    longest = extent.index(max(extent))
    spot[longest] = (spot[longest] + 1) % extent[longest]
    return entries.at[tuple(spot)].set(largest)


def shard_levels(stream_key, shape, cuts, low, top_value):
    def one(dim, blocks):
        draws = jax.random.uniform(jax.random.fold_in(jax.random.fold_in(stream_key, 6), dim), (blocks,), jnp.float32, low / len(cuts), top_value / len(cuts))
        return jnp.repeat(jnp.exp(draws), shape[dim] // blocks).reshape((-1,) + (1,) * (len(shape) - dim - 1))

    level = one(*cuts[0])
    for cut in cuts[1:]:
        level = level * one(*cut)
    return level


def deal_out(stream_key, own, number, rows, amount, top, bound, lean):
    sequence = jax.random.permutation(stream_key, amount)
    heavy_load, usual = portions_of(amount, rows * top, bound, lean, True), portions_of(amount, rows * top, bound, lean, False)
    places = jnp.arange(amount)

    def named(lengths, rotation):
        used = int((lengths > 0).sum())
        fixed = max(1, used // 4)
        moved = fixed + (places - fixed + rotation * (used - fixed)) % max(1, amount - fixed)
        return jnp.zeros((amount,), jnp.int32).at[sequence[jnp.where(places < fixed, places, moved)]].set(jnp.asarray(lengths, jnp.int32))

    lengths = jnp.where(number % 4 == 0, named(heavy_load, number // 4), named(usual, number - number // 4 - 1))
    mixed = jax.random.permutation(jax.random.fold_in(own, 3), amount)
    giver, sink = mixed[0:amount // 2 * 2:2], mixed[1:amount // 2 * 2:2]
    slack = jnp.minimum(lengths[giver] - 1, bound - lengths[sink]) // 2
    slack = jnp.where((giver == sequence[0]) | (sink == sequence[0]) | (lengths[sink] == 0), 0, jnp.maximum(slack, 0))
    moved = jax.random.randint(jax.random.fold_in(own, 4), (amount // 2,), 0, 1 << 20) % (slack + 1)
    lengths = lengths.at[giver].add(-moved).at[sink].add(moved)
    items = jnp.searchsorted(jnp.cumsum(lengths), jnp.arange(rows * top), side="right").astype(jnp.int32)
    table = items.reshape(top, rows).T
    table = table[jax.random.permutation(jax.random.fold_in(own, 1), rows)]
    rotation = jax.random.randint(jax.random.fold_in(own, 2), (rows, 1), 0, top)
    return jnp.take_along_axis(table, (jnp.arange(top)[None, :] + rotation) % top, axis=1)


def portions_of(amount, total, most, skew, full):
    weights = [(1 << 20) // math.isqrt(rank ** skew) + 1 for rank in range(1, amount + 1)]
    largest = most if full else min(most, max(-(-total // amount), total * weights[0] // sum(weights)))
    least = 1 if total - largest >= amount - 1 else 0
    holding, spare = [largest] + [least] * (amount - 1), total - largest - least * (amount - 1)
    while spare > 0:
        candidates = [i for i in range(1, amount) if holding[i] < largest] or [i for i in range(1, amount) if holding[i] < most]
        whole, remaining = sum([weights[i] for i in candidates]), spare
        for i in candidates:
            more = min(most - holding[i], max(1, remaining * weights[i] // whole), spare)
            holding[i] = holding[i] + more
            spare = spare - more
    return np.array(holding)


def gaussian(stream_key, shape, spread, bound, cuts=(), kind=jnp.bfloat16):
    entries = spread * jax.random.normal(stream_key, shape, jnp.float32)
    if cuts:
        entries = entries * shard_levels(stream_key, shape, cuts, -0.22, 0.18)
    return jnp.clip(entries, -bound, bound).astype(kind)


def setup_inputs(seed: int = 0) -> dict:
    key_of = jax.random.split(jax.random.key(seed), 12)
    air_temp = gaussian(key_of[0], (G, NL, PW), 1.0, 6.0, ((0, 8), (1, 16)), jnp.float32)
    air_vel = jnp.clip(jax.random.uniform(key_of[1], (G, NL, PW), jnp.float32, -0.3, 0.3) * shard_levels(key_of[1], (G, NL, PW), ((0, 8), (1, 16)), -0.4, 0.0), -0.3, 0.3)
    air_kappa = jnp.clip(jnp.exp(math.log(0.2) - 2.3025851 * jax.random.uniform(key_of[2], (G, NL, PW), jnp.float32) ** shard_levels(key_of[2], (G, NL, PW), ((0, 8), (1, 16)), -0.2, 0.2)), 0.02, 0.2)
    group_width = set_ends(jax.random.randint(key_of[3], (G,), PW // 4, PW + 1), jax.random.fold_in(key_of[3], 1), PW // 4, PW).astype(jnp.int32)
    sub_temp = gaussian(key_of[4], (NBLK, NODES), 1.0, 6.0, ((0, 128),), jnp.float32)
    sub_coupling = gaussian(key_of[5], (NBLK, NNB, NODES * NODES), (4 * NNB * NODES) ** -0.5, 0.1875, ((0, 128),))
    neighbors = draw_neighbors(jax.random.fold_in(key_of[11], 71), 0)
    iface_count = set_ends(jax.random.randint(key_of[7], (DEVICES,), 3 * IROWS // 4, IROWS + 1), jax.random.fold_in(key_of[7], 1), 3 * IROWS // 4, IROWS).astype(jnp.int32)
    iface_seg = draw_iface_seg(jax.random.fold_in(key_of[11], 71), 0)
    iface_owner_keys = jax.random.split(jax.random.fold_in(key_of[9], 1), (DEVICES * IROWS) // IROWS)
    iface_owner_turns = jax.random.permutation(jax.random.fold_in(key_of[9], 3), (DEVICES * IROWS) // IROWS)
    iface_owner = jax.vmap(lambda own, number: deal_out(jax.random.fold_in(key_of[9], 2), own, number, IROWS, DEVICES, 1, CAP, 2))(iface_owner_keys, iface_owner_turns).reshape((DEVICES * IROWS, 1))
    iface_block = set_ends(jax.random.randint(key_of[10], (DEVICES * IROWS,), 0, BDEV), jax.random.fold_in(key_of[10], 1), 0, BDEV - 1).astype(jnp.int32)
    return dict(air_temp=air_temp, air_vel=air_vel, air_kappa=air_kappa, group_width=group_width, sub_temp=sub_temp, sub_coupling=sub_coupling, neighbors=neighbors, iface_count=iface_count, iface_seg=iface_seg, iface_owner=iface_owner, iface_block=iface_block)


uptake = 0.3
release = 0.5


def advance(field, vel, kappa, live):
    east = jnp.roll(field, -1, axis=1)
    west = jnp.roll(field, 1, axis=1)
    north = jnp.concatenate([field[:, :, 1:], field[:, :, -1:]], axis=2)
    south = jnp.concatenate([field[:, :, :1], field[:, :, :-1]], axis=2)
    fresh = field + kappa * (east + west - 2.0 * field) + kappa * (north + south - 2.0 * field) - 0.5 * vel * (east - west)
    return jnp.where(live, fresh, field)


def to_rows(air):
    spans = NL // CA
    cube = air.reshape(G, spans, CA, PW).transpose(1, 0, 2, 3)
    return cube.reshape(DEVICES, NSEG, NODES)


def from_rows(rows):
    spans = NL // CA
    cube = rows.reshape(spans, G, CA, PW).transpose(1, 0, 2, 3)
    return cube.reshape(G, NL, PW)


def reference(air_temp, air_vel, air_kappa, group_width, sub_temp, sub_coupling, neighbors, iface_count, iface_seg, iface_owner, iface_block):
    live = (jnp.arange(PW, dtype=jnp.int32)[None, None, :] < group_width[:, None, None])
    field = air_temp
    for step in range(STEPS):
        field = advance(field, air_vel, air_kappa, live)
    rows_in = to_rows(air_temp)
    seg = iface_seg.reshape(DEVICES, IROWS)
    air_rows = jnp.take_along_axis(rows_in, seg[:, :, None], axis=1)
    active = (jnp.arange(IROWS, dtype=jnp.int32)[None, :] < iface_count[:, None]).reshape(-1)
    air_rows = air_rows.reshape(-1, NODES)
    target = iface_owner[:, 0] * BDEV + iface_block
    gain = jnp.where(active[:, None], uptake * (air_rows - sub_temp[target]), jnp.float32(0.0))
    substrate = sub_temp.at[target].add(gain)
    coupling = sub_coupling.reshape(DEVICES, BDEV, NNB, NODES, NODES)
    links = neighbors.reshape(DEVICES, BDEV, NNB)
    for step in range(SSTEPS):
        rounded = substrate.astype(jnp.bfloat16)

        def one(pair):
            blocks, idx = pair
            near = rounded[idx].astype(jnp.float32)
            return jnp.einsum("bkij,bkj->bi", blocks.astype(jnp.float32), near)

        added = lax.map(one, (coupling, links)).reshape(NBLK, NODES)
        substrate = substrate + added
    surface = substrate[target]
    delta = jnp.where(active[:, None], release * (surface - air_rows), jnp.float32(0.0)).reshape(DEVICES, IROWS, NODES)
    rows_out = to_rows(field)
    place = jnp.arange(DEVICES, dtype=jnp.int32)[:, None]
    rows_out = rows_out.at[place, seg].add(delta)
    return from_rows(rows_out), substrate
```

```python
import jax
import jax.numpy as jnp
from jax import lax
from jax.sharding import PartitionSpec as P

STEPS = 4
SSTEPS = 2
NODES = 64


uptake = 0.3
release = 0.5


def with_halo(block, sides, width, periodic):
    for axis, dim in sides:
        count = lax.axis_size(axis)
        forward = [(i, i + 1) for i in range(count - 1)]
        if periodic:
            forward.append((count - 1, 0))
        backward = [(target, source) for source, target in forward]
        low = lax.ppermute(
            lax.slice_in_dim(block, block.shape[dim] - width, None, axis=dim), axis, forward
        )
        high = lax.ppermute(lax.slice_in_dim(block, 0, width, axis=dim), axis, backward)
        block = jnp.concatenate([low, block, high], axis=dim)
    return block


def advance(padded, vel, kappa, live):
    centre = padded[:, 1:-1]
    east = padded[:, 2:]
    west = padded[:, :-2]
    north = jnp.concatenate([centre[:, :, 1:], centre[:, :, -1:]], axis=2)
    south = jnp.concatenate([centre[:, :, :1], centre[:, :, :-1]], axis=2)
    fresh = (
        centre
        + kappa * (east + west - 2.0 * centre)
        + kappa * (north + south - 2.0 * centre)
        - 0.5 * vel * (east - west)
    )
    return jnp.where(live, fresh, centre)


def per_device(
    air_temp,
    air_vel,
    air_kappa,
    group_width,
    sub_temp,
    sub_coupling,
    neighbors,
    iface_count,
    iface_seg,
    iface_owner,
    iface_block,
):
    width = air_temp.shape[2]
    live = (jnp.arange(width, dtype=jnp.int32) < group_width[0])[None, None, :]
    field = air_temp
    for step in range(STEPS):
        padded = with_halo(field, (("span", 1),), 1, True)
        field = advance(padded, air_vel, air_kappa, live)
    devices = lax.axis_size(("span", "group"))
    groups = lax.axis_size("group")
    here = lax.axis_index("span") * groups + lax.axis_index("group")
    irows = iface_seg.shape[0]
    capacity = max(2, 2 * irows // devices)
    air_rows = air_temp.reshape(-1, NODES)[iface_seg]
    owner = iface_owner[:, 0]
    active = jnp.arange(irows, dtype=jnp.int32) < iface_count[0]
    onehot = (owner[:, None] == jnp.arange(devices, dtype=jnp.int32)[None, :]).astype(jnp.int32)
    slot = jnp.sum((jnp.cumsum(onehot, axis=0) - onehot) * onehot, axis=1)
    place = owner * capacity + slot
    send_rows = (
        jnp.zeros((devices * capacity, NODES), jnp.float32)
        .at[place]
        .set(jnp.where(active[:, None], air_rows, jnp.float32(0.0)))
    )
    send_index = (
        jnp.full((devices * capacity,), -1, jnp.int32)
        .at[place]
        .set(jnp.where(active, iface_block, -1))
    )
    recv_rows = lax.all_to_all(
        send_rows, ("span", "group"), split_axis=0, concat_axis=0, tiled=True
    )
    recv_index = lax.all_to_all(
        send_index, ("span", "group"), split_axis=0, concat_axis=0, tiled=True
    )
    valid = recv_index >= 0
    target = jnp.maximum(recv_index, 0)
    gain = jnp.where(valid[:, None], uptake * (recv_rows - sub_temp[target]), jnp.float32(0.0))
    substrate = sub_temp.at[target].add(gain)
    blocks = substrate.shape[0]
    links_count = sub_coupling.shape[1]
    coupling = sub_coupling.reshape(blocks, links_count, NODES, NODES)
    local_links = neighbors - (here - 1) * blocks
    for step in range(SSTEPS):
        rounded = substrate.astype(jnp.bfloat16)
        beside_all = with_halo(rounded, ((("span", "group"), 0),), blocks, False)
        near = beside_all[local_links]
        substrate = substrate + jnp.einsum(
            "bkij,bkj->bi", coupling, near, preferred_element_type=jnp.float32
        )
    reply = substrate[target]
    returned = lax.all_to_all(reply, ("span", "group"), split_axis=0, concat_axis=0, tiled=True)
    surface = returned[place]
    delta = jnp.where(active[:, None], release * (surface - air_rows), jnp.float32(0.0))
    final = field.reshape(-1, NODES).at[iface_seg].add(delta, unique_indices=True)
    return (final.reshape(field.shape), substrate)


def solution(mesh):
    placed = (
        P("group", "span", None),
        P("group", "span", None),
        P("group", "span", None),
        P("group"),
        P(("span", "group"), None),
        P(("span", "group"), None, None),
        P(("span", "group"), None),
        P(("span", "group")),
        P(("span", "group")),
        P(("span", "group"), None),
        P(("span", "group")),
    )
    return jax.shard_map(
        per_device,
        mesh=mesh,
        in_specs=placed,
        out_specs=(P("group", "span", None), P(("span", "group"), None)),
        check_vma=False,
    )
```

```python
import functools

import jax
import jax.numpy as jnp
from jax import lax
from jax.experimental import pallas as pl
from jax.experimental.pallas import tpu as pltpu
from jax.sharding import PartitionSpec as P

STEPS = 4
SSTEPS = 2
NODES = 64
CAP = 16
LANES = 128
UPTAKE = 0.3
RELEASE = 0.5
MESH = pl.DeviceIdType.MESH
F32 = jnp.float32
BF16 = jnp.bfloat16
I32 = jnp.int32


def iota(shape, dim):
    return lax.broadcasted_iota(I32, shape, dim)


def onehot(mask):
    return jnp.where(mask, F32(1.0), F32(0.0)).astype(BF16)


def mm(a, b):
    return jnp.dot(a, b, preferred_element_type=F32)


def mm_nt(a, b):
    return lax.dot_general(a, b, (((1,), (1,)), ((), ())), preferred_element_type=F32)


def split(x):
    hi = x.astype(BF16)
    lo = (x - hi.astype(F32)).astype(BF16)
    return hi, lo


def kernel(
    nspan,
    ngroup,
    air_h,
    vel_h,
    kap_h,
    width_s,
    sub_h,
    c_h,
    nbr_h,
    count_s,
    seg_h,
    own_h,
    blk_h,
    air_o,
    sub_o,
    air_v,
    vel_v,
    kap_v,
    sub_v,
    c_v,
    nbr_v,
    seg_v,
    own_v,
    blk_v,
    field,
    bank,
    pick,
    send,
    recv,
    back,
    got,
    idx_out,
    idx_in,
    t_v,
    tt_v,
    pt_v,
    st_v,
    near_map,
    near_v,
    z_v,
    beside,
    edge_lo,
    edge_hi,
    halo_w,
    halo_e,
    in_sem,
    send_sem,
    recv_sem,
    edge_send,
    edge_recv,
    side_send,
    side_recv,
):
    ndev = nspan * ngroup
    span = lax.axis_index("span")
    group = lax.axis_index("group")
    me = span * ngroup + group

    def where_is(d):
        return (d // ngroup, d % ngroup)

    loads = []
    for k, (src, dst) in enumerate(
        (
            (own_h, own_v),
            (seg_h, seg_v),
            (blk_h, blk_v),
            (air_h, air_v),
            (nbr_h, nbr_v),
            (sub_h, sub_v),
            (vel_h, vel_v),
            (kap_h, kap_v),
            (c_h, c_v),
        )
    ):
        copy = pltpu.make_async_copy(src, dst, in_sem.at[k])
        copy.start()
        loads.append(copy)

    barrier = pltpu.get_barrier_semaphore()

    @pl.loop(1, ndev)
    def _(i):
        pl.semaphore_signal(
            barrier, inc=1, device_id=where_is((me + i) % ndev), device_id_type=MESH
        )

    count = count_s[0]
    width = width_s[0]
    lane = iota((1, LANES), 1)

    for k in range(3):
        loads[k].wait()
    own8 = own_v[...]
    seg8 = seg_v[...]
    blk8 = blk_v[...]
    active8 = (iota((8, LANES), 0) * LANES + iota((8, LANES), 1)) < count
    sub128 = iota((LANES, LANES), 0)
    hits = [own8[c : c + 1, :] == sub128 for c in range(8)]
    upper = onehot(iota((LANES, 2 * LANES), 0) < iota((LANES, 2 * LANES), 1))
    ahead = mm(jnp.concatenate([onehot(h) for h in hits], axis=0), upper)
    carry = jnp.zeros((LANES, LANES), F32)
    ranks = []
    for c in range(8):
        part = ahead[c * LANES : (c + 1) * LANES]
        ranks.append(
            jnp.sum(jnp.where(hits[c], part[:, :LANES] + carry, F32(0.0)), axis=0, keepdims=True)
        )
        carry = carry + part[:, LANES:]
    rank8 = jnp.concatenate(ranks, axis=0)
    place8 = jnp.where(active8, own8 * CAP + rank8.astype(I32), -1)
    line8 = seg8 // LANES
    key8 = (line8 // 8) * 512 + ((seg8 % LANES) // 2) * 8 + line8 % 8
    half8 = seg8 % 2
    shift8 = jnp.where(active8, rank8.astype(I32) + (me % 8) * CAP, -1)
    table = jnp.concatenate(
        [
            place8.astype(F32),
            key8.astype(F32),
            half8.astype(F32),
            shift8.astype(F32),
            (blk8 + 1).astype(F32),
            active8.astype(F32),
            jnp.zeros((LANES - 48, LANES), F32),
        ],
        axis=0,
    )
    columns = table.T.astype(I32)

    def column(a, c):
        return columns[:, a * 8 + c : a * 8 + c + 1]

    slots = jnp.concatenate(
        [
            jnp.where(column(3, c) == lane, column(4, c).astype(F32), F32(0.0)).astype(BF16)
            for c in range(8)
        ],
        axis=0,
    )
    owners = jnp.concatenate([onehot(h) for h in hits], axis=1)
    idx_out[...] = mm(owners, slots)

    loads[3].wait()
    for line in range(2):
        for j in range(64):
            k = (line * 64 + j) * 8
            a = air_v[line * 8 : line * 8 + 8, j * LANES : (j + 1) * LANES]
            hi = a.astype(BF16).astype(F32)
            lo = a - hi
            z_v[k : k + 8, :LANES] = jnp.where(lane < 64, hi, pltpu.roll(lo, 64, 1))
            z_v[k : k + 8, LANES:] = jnp.where(lane < 64, pltpu.roll(hi, 64, 1), lo)
    bank[...] = z_v[...].astype(BF16)
    key_lane = iota((LANES, 8 * LANES), 1)
    for c in range(8):
        rows = mm(onehot(column(1, c) == key_lane), bank[...])
        pick[c * LANES : (c + 1) * LANES, :] = jnp.where(
            column(2, c) == 0, rows[:, :LANES], rows[:, LANES:]
        ).astype(BF16)

    @pl.loop(0, 8)
    def _(q):
        slot = iota((256, LANES), 0) + q * 256
        sel = jnp.concatenate([onehot(place8[c : c + 1, :] == slot) for c in range(8)], axis=1)
        send[pl.ds(q * 16, 16)] = mm(sel, pick[...]).astype(BF16).reshape(16, CAP, LANES)

    edge_lo[0] = air_v[0:1, :]
    edge_hi[0] = air_v[15:16, :]
    field[:, LANES : LANES + 8192] = air_v[...]

    def pad_ends():
        field[:, :LANES] = jnp.broadcast_to(field[:, LANES : LANES + 1], (16, LANES))
        field[:, LANES + 8192 :] = jnp.broadcast_to(
            field[:, LANES + 8191 : LANES + 8192], (16, LANES)
        )

    pad_ends()

    pl.semaphore_wait(barrier, ndev - 1)

    def edges(step):
        east = ((span + 1) % nspan, group)
        west = ((span + nspan - 1) % nspan, group)
        return (
            pltpu.make_async_remote_copy(
                edge_hi.at[step], halo_w.at[step], edge_send.at[step, 0], edge_recv.at[step, 0],
                device_id=east, device_id_type=MESH,
            ),
            pltpu.make_async_remote_copy(
                edge_lo.at[step], halo_e.at[step], edge_send.at[step, 1], edge_recv.at[step, 1],
                device_id=west, device_id_type=MESH,
            ),
        )

    for e in edges(0):
        e.start()

    def scatter_all(src, dst, k):
        @pl.loop(1, ndev)
        def _(i):
            d = (me + i) % ndev
            pltpu.make_async_remote_copy(
                src.at[d], dst.at[me], send_sem.at[k], recv_sem.at[k],
                device_id=where_is(d), device_id_type=MESH,
            ).start()

    def whole(src, dst, k):
        return pltpu.make_async_remote_copy(
            src.at[pl.ds(0, ndev - 1)], dst.at[pl.ds(0, ndev - 1)], send_sem.at[k], recv_sem.at[k],
            device_id=where_is((me + 1) % ndev), device_id_type=MESH,
        )

    scatter_all(send, recv, 0)
    scatter_all(idx_out, idx_in, 1)
    recv[me] = send[me]
    idx_in[pl.ds(me, 1), :] = idx_out[pl.ds(me, 1), :]

    for c in range(8):
        slot_lane = iota((LANES, 2048), 1)
        pt_v[c * LANES : (c + 1) * LANES, :] = onehot(column(0, c) == slot_lane)

    @pl.loop(0, 8)
    def _(q):
        at = iota((LANES, LANES), 0) + q * LANES
        st_v[pl.ds(q * LANES, LANES), :] = jnp.concatenate(
            [onehot(key8[c : c + 1, :] == at) for c in range(8)], axis=1
        )

    loads[4].wait()
    nbr = (nbr_v[...] - (me - 1) * LANES).astype(F32)
    nbr8 = jnp.concatenate([nbr, nbr], axis=0)

    @pl.loop(0, 8)
    def _(q):
        tiled = jnp.concatenate([nbr8] * 16, axis=0)
        own_lane = (iota((LANES, LANES), 0) // 8 + q * 16) == iota((LANES, LANES), 1)
        link = jnp.sum(jnp.where(own_lane, tiled, F32(0.0)), axis=1, keepdims=True).astype(I32)
        near_map[pl.ds(q * LANES, LANES), :] = onehot(link == iota((LANES, 3 * LANES), 1))

    loads[6].wait()
    loads[7].wait()

    def advance(step):
        for e in edges(step):
            e.wait()
        wide = 1024
        row = iota((16, wide), 0)
        fresh = []
        for j in range(8192 // wide):
            ext = field[:, j * wide : j * wide + wide + 2 * LANES]
            t = ext[:, LANES : LANES + wide]
            north = pltpu.roll(ext, wide + 2 * LANES - 1, 1)[:, LANES : LANES + wide]
            south = pltpu.roll(ext, 1, 1)[:, LANES : LANES + wide]
            cut = slice(j * wide, (j + 1) * wide)
            east = jnp.where(row == 15, halo_e[step, :, cut], pltpu.roll(t, 15, 0))
            west = jnp.where(row == 0, halo_w[step, :, cut], pltpu.roll(t, 1, 0))
            new = (
                t
                + kap_v[:, cut] * ((east + west) + (north + south) - 4.0 * t)
                - (0.5 * vel_v[:, cut]) * (east - west)
            )
            new = jnp.where(iota((16, wide), 1) + j * wide < width, new, t)
            air_v[:, cut] = new
        field[:, LANES : LANES + 8192] = air_v[...]
        if step + 1 < STEPS:
            pad_ends()
            edge_lo[step + 1] = air_v[0:1, :]
            edge_hi[step + 1] = air_v[15:16, :]
            for e in edges(step + 1):
                e.start()

    advance(0)

    loads[5].wait()
    sub = jnp.concatenate([sub_v[...], sub_v[...]], axis=0).T
    both = whole(idx_out, idx_in, 1)
    both.wait_send()
    both.wait_recv()
    for q in range(16):
        at = jnp.sum(idx_in[q * 8 : q * 8 + 8, :], axis=0, keepdims=True).astype(I32)
        t_q = jnp.where(at == iota((LANES, LANES), 0) + 1, F32(1.0), F32(0.0))
        t_v[:, q * LANES : (q + 1) * LANES] = t_q.astype(BF16)
        tt_v[q * LANES : (q + 1) * LANES, :] = t_q.T.astype(BF16)
    hits_b = mm(t_v[...], jnp.ones((2048, LANES), BF16))
    both = whole(send, recv, 0)
    both.wait_send()
    both.wait_recv()
    total = mm(t_v[...], recv[...].reshape(2048, LANES))
    total = total + pltpu.roll(total, 64, 1)
    sub = sub + UPTAKE * (total - hits_b * sub)

    def sides(step):
        nxt = where_is((me + 1) % ndev)
        prev = where_is((me + ndev - 1) % ndev)
        return (
            pltpu.make_async_remote_copy(
                beside.at[step, 1], beside.at[step, 0], side_send.at[step, 0], side_recv.at[step, 0],
                device_id=nxt, device_id_type=MESH,
            ),
            pltpu.make_async_remote_copy(
                beside.at[step, 1], beside.at[step, 2], side_send.at[step, 1], side_recv.at[step, 1],
                device_id=prev, device_id_type=MESH,
            ),
        )

    lane2 = iota((LANES, LANES), 1)
    row2 = iota((LANES, LANES), 0)
    gather_i = onehot((lane2 % 64) // 2 == row2 // 4)
    gather_i = jnp.concatenate([gather_i, gather_i], axis=0)
    per_block = onehot(iota((LANES, 8 * LANES), 1) // 8 == iota((LANES, 8 * LANES), 0))
    half_lane = (iota((8 * LANES, LANES), 0) % 8) // 4 == iota((8 * LANES, LANES), 1) // 64
    odd_lane = (iota((8 * LANES, LANES), 0) % 8) // 4 == iota((8 * LANES, LANES), 1) % 2
    same = iota((8, LANES), 0) % 4 == iota((8, LANES), 1) % 4

    for step in range(SSTEPS):
        beside[step, 1] = sub.astype(BF16)
        for s in sides(step):
            s.start()
        advance(step + 1)
        if step == 0:
            loads[8].wait()
        for s in sides(step):
            s.wait()
        near = mm(near_map[...], beside[step].reshape(3 * LANES, LANES))
        near_v[...] = jnp.where(half_lane, near, F32(0.0)).astype(BF16)

        @pl.loop(0, 64, unroll=8)
        def _(p):
            res = mm_nt(near_v[pl.ds(p * 16, 16), :], c_v[pl.ds(p * 256, 256), :])
            z_v[pl.ds(p * 16, 8), :LANES] = jnp.where(same, res[:8, :LANES], F32(0.0))
            z_v[pl.ds(p * 16 + 8, 8), :LANES] = jnp.where(same, res[8:, LANES:], F32(0.0))

        hi, lo = split(z_v[:, :LANES])
        w = mm(jnp.concatenate([hi, lo], axis=1), gather_i)
        hi, lo = split(jnp.where(odd_lane, w, F32(0.0)))
        added = mm(per_block, jnp.concatenate([hi, lo], axis=1))
        sub = sub + (added[:, :LANES] + added[:, LANES:])

    hi = sub.astype(BF16).astype(F32)
    pair = jnp.where(lane2 < 64, hi, sub - hi).astype(BF16)
    back[...] = mm(tt_v[...], pair).astype(BF16).reshape(ndev, CAP, LANES)
    scatter_all(back, got, 2)
    got[me] = back[me]
    sub_o[...] = sub.T[:64, :]
    advance(3)
    both = whole(back, got, 2)
    both.wait_send()
    both.wait_recv()

    for c in range(8):
        rows = slice(c * LANES, (c + 1) * LANES)
        surf = mm(pt_v[rows, :], got[...].reshape(2048, LANES))
        gap = surf - pick[rows, :].astype(F32)
        gap = RELEASE * (gap + pltpu.roll(gap, 64, 1))
        keep = jnp.logical_and(column(5, c) == 1, column(2, c) == lane2 // 64)
        hi, lo = split(jnp.where(keep, gap, F32(0.0)))
        bank[rows, :LANES] = hi
        bank[rows, LANES:] = lo
    z_v[...] = mm(st_v[...], bank[...])
    for line in range(2):
        for j in range(64):
            k = (line * 64 + j) * 8
            cut = slice(j * LANES, (j + 1) * LANES)
            air_o[line * 8 : line * 8 + 8, cut] = air_v[line * 8 : line * 8 + 8, cut] + (
                z_v[k : k + 8, :LANES] + z_v[k : k + 8, LANES:]
            )


def per_device(
    nspan,
    ngroup,
    air_temp,
    air_vel,
    air_kappa,
    group_width,
    sub_temp,
    sub_coupling,
    neighbors,
    iface_count,
    iface_seg,
    iface_owner,
    iface_block,
):
    cells, section = air_temp.shape[1:]
    blocks, links, _ = sub_coupling.shape
    coupling = (
        sub_coupling.reshape(blocks, links, 32, LANES)
        .transpose(0, 2, 1, 3)
        .reshape(blocks * links * 32, LANES)
    )
    ndev = nspan * ngroup
    vmem = pltpu.VMEM
    dma = pltpu.SemaphoreType.DMA
    any_space = pl.BlockSpec(memory_space=pl.ANY)
    smem = pl.BlockSpec(memory_space=pltpu.SMEM)
    in_vmem = pl.BlockSpec(memory_space=pltpu.VMEM)
    air, sub = pl.pallas_call(
        functools.partial(kernel, nspan, ngroup),
        out_shape=(
            jax.ShapeDtypeStruct((cells, section), F32),
            jax.ShapeDtypeStruct((NODES, blocks), F32),
        ),
        in_specs=[any_space] * 3 + [smem] + [any_space] * 3 + [smem] + [any_space] * 3,
        out_specs=(in_vmem, in_vmem),
        scratch_shapes=[
            vmem((cells, section), F32),
            vmem((cells, section), F32),
            vmem((cells, section), F32),
            vmem((NODES, blocks), F32),
            vmem(coupling.shape, BF16),
            vmem((links, blocks), I32),
            vmem((8, LANES), I32),
            vmem((8, LANES), I32),
            vmem((8, LANES), I32),
            vmem((cells, section + 2 * LANES), F32),
            vmem((8 * LANES, 2 * LANES), BF16),
            vmem((8 * LANES, LANES), BF16),
            vmem((ndev, CAP, LANES), BF16),
            vmem((ndev, CAP, LANES), BF16),
            vmem((ndev, CAP, LANES), BF16),
            vmem((ndev, CAP, LANES), BF16),
            vmem((ndev, LANES), F32),
            vmem((ndev, LANES), F32),
            vmem((LANES, ndev * CAP), BF16),
            vmem((ndev * CAP, LANES), BF16),
            vmem((8 * LANES, ndev * CAP), BF16),
            vmem((8 * LANES, 8 * LANES), BF16),
            vmem((8 * LANES, 3 * LANES), BF16),
            vmem((8 * LANES, LANES), BF16),
            vmem((8 * LANES, 2 * LANES), F32),
            vmem((SSTEPS, 3, LANES, LANES), BF16),
            vmem((STEPS, 1, section), F32),
            vmem((STEPS, 1, section), F32),
            vmem((STEPS, 1, section), F32),
            vmem((STEPS, 1, section), F32),
            dma((9,)),
            dma((3,)),
            dma((3,)),
            dma((STEPS, 2)),
            dma((STEPS, 2)),
            dma((SSTEPS, 2)),
            dma((SSTEPS, 2)),
        ],
        compiler_params=pltpu.CompilerParams(
            collective_id=0, has_side_effects=True, vmem_limit_bytes=56 << 20
        ),
    )(
        air_temp.reshape(cells, section),
        air_vel.reshape(cells, section),
        air_kappa.reshape(cells, section),
        group_width,
        sub_temp.T,
        coupling,
        neighbors.T,
        iface_count,
        iface_seg.reshape(8, LANES),
        iface_owner.reshape(8, LANES),
        iface_block.reshape(8, LANES),
    )
    return air.reshape(1, cells, section), sub.T


def solution(mesh):
    placed = (
        P("group", "span", None),
        P("group", "span", None),
        P("group", "span", None),
        P("group"),
        P(("span", "group"), None),
        P(("span", "group"), None, None),
        P(("span", "group"), None),
        P(("span", "group")),
        P(("span", "group")),
        P(("span", "group"), None),
        P(("span", "group")),
    )
    return jax.shard_map(
        functools.partial(per_device, mesh.shape["span"], mesh.shape["group"]),
        mesh=mesh,
        in_specs=placed,
        out_specs=(P("group", "span", None), P(("span", "group"), None)),
        check_vma=False,
    )
```

```python
import functools

import jax
import jax.numpy as jnp
from jax import lax
from jax.experimental import pallas as pl
from jax.experimental.pallas import tpu as pltpu
from jax.sharding import PartitionSpec as P

STEPS = 4
SSTEPS = 2
NODES = 64
CAP = 16
LANES = 128
UPTAKE = 0.3
RELEASE = 0.5
MESH = pl.DeviceIdType.MESH
F32 = jnp.float32
BF16 = jnp.bfloat16
I32 = jnp.int32


def iota(shape, dim):
    return lax.broadcasted_iota(I32, shape, dim)


def onehot(mask):
    return jnp.where(mask, F32(1.0), F32(0.0)).astype(BF16)


def mm(a, b):
    return jnp.dot(a, b, preferred_element_type=F32)


def mm_nt(a, b):
    return lax.dot_general(a, b, (((1,), (1,)), ((), ())), preferred_element_type=F32)


def split(x):
    hi = x.astype(BF16)
    lo = (x - hi.astype(F32)).astype(BF16)
    return hi, lo


def kernel(
    nspan,
    ngroup,
    air_h,
    vel_h,
    kap_h,
    width_s,
    sub_h,
    c_h,
    nbr_h,
    count_s,
    seg_h,
    own_h,
    blk_h,
    air_o,
    sub_o,
    air_v,
    vel_v,
    kap_v,
    sub_v,
    c_v,
    nbr_v,
    seg_v,
    own_v,
    blk_v,
    field,
    bank,
    pick,
    send,
    recv,
    back,
    got,
    idx_out,
    idx_row_in,
    idx_mid,
    idx_in,
    t_v,
    tt_v,
    pt_v,
    st_v,
    near_map,
    near_v,
    z_v,
    beside,
    edge_lo,
    edge_hi,
    halo_w,
    halo_e,
    in_sem,
    send_sem,
    recv_sem,
    edge_send,
    edge_recv,
    side_send,
    side_recv,
    ready,
):
    ndev = nspan * ngroup
    span = lax.axis_index("span")
    group = lax.axis_index("group")
    me = span * ngroup + group

    def where_is(d):
        return (d // ngroup, d % ngroup)

    loads = []
    for k, (src, dst) in enumerate(
        (
            (own_h, own_v),
            (seg_h, seg_v),
            (blk_h, blk_v),
            (air_h, air_v),
            (nbr_h, nbr_v),
            (sub_h, sub_v),
            (vel_h, vel_v),
            (kap_h, kap_v),
            (c_h, c_v),
        )
    ):
        copy = pltpu.make_async_copy(src, dst, in_sem.at[k])
        copy.start()
        loads.append(copy)

    barrier = pltpu.get_barrier_semaphore()

    row_peers = [(span, (group + j) % ngroup) for j in range(ngroup)]
    column_peers = [((span + i) % nspan, group) for i in range(nspan)]
    for peer in row_peers[1:] + column_peers[1:]:
        pl.semaphore_signal(barrier, inc=1, device_id=peer, device_id_type=MESH)

    count = count_s[0]
    width = width_s[0]
    lane = iota((1, LANES), 1)

    for k in range(3):
        loads[k].wait()
    own8 = own_v[...]
    seg8 = seg_v[...]
    blk8 = blk_v[...]
    active8 = (iota((8, LANES), 0) * LANES + iota((8, LANES), 1)) < count
    sub128 = iota((LANES, LANES), 0)
    hits = [own8[c : c + 1, :] == sub128 for c in range(8)]
    upper = onehot(iota((LANES, 2 * LANES), 0) < iota((LANES, 2 * LANES), 1))
    ahead = mm(jnp.concatenate([onehot(h) for h in hits], axis=0), upper)
    carry = jnp.zeros((LANES, LANES), F32)
    ranks = []
    for c in range(8):
        part = ahead[c * LANES : (c + 1) * LANES]
        ranks.append(
            jnp.sum(jnp.where(hits[c], part[:, :LANES] + carry, F32(0.0)), axis=0, keepdims=True)
        )
        carry = carry + part[:, LANES:]
    rank8 = jnp.concatenate(ranks, axis=0)
    place8 = jnp.where(active8, own8 * CAP + rank8.astype(I32), -1)
    line8 = seg8 // LANES
    key8 = (line8 // 8) * 512 + ((seg8 % LANES) // 2) * 8 + line8 % 8
    half8 = seg8 % 2
    shift8 = jnp.where(active8, rank8.astype(I32) + group * CAP, -1)
    table = jnp.concatenate(
        [
            place8.astype(F32),
            key8.astype(F32),
            half8.astype(F32),
            shift8.astype(F32),
            (blk8 + 1).astype(F32),
            active8.astype(F32),
            jnp.zeros((LANES - 48, LANES), F32),
        ],
        axis=0,
    )
    columns = table.T.astype(I32)

    def column(a, c):
        return columns[:, a * 8 + c : a * 8 + c + 1]

    slots = jnp.concatenate(
        [
            jnp.where(column(3, c) == lane, column(4, c).astype(F32), F32(0.0)).astype(BF16)
            for c in range(8)
        ],
        axis=0,
    )
    spot8 = (own8 % ngroup) * nspan + own8 // ngroup
    owners = jnp.concatenate([onehot(spot8[c : c + 1, :] == sub128) for c in range(8)], axis=1)
    idx_out[...] = mm(owners, slots)

    loads[3].wait()
    for line in range(2):
        for j in range(64):
            k = (line * 64 + j) * 8
            a = air_v[line * 8 : line * 8 + 8, j * LANES : (j + 1) * LANES]
            hi = a.astype(BF16).astype(F32)
            lo = a - hi
            z_v[k : k + 8, :LANES] = jnp.where(lane < 64, hi, pltpu.roll(lo, 64, 1))
            z_v[k : k + 8, LANES:] = jnp.where(lane < 64, pltpu.roll(hi, 64, 1), lo)
    bank[...] = z_v[...].astype(BF16)
    key_lane = iota((LANES, 8 * LANES), 1)
    for c in range(8):
        rows = mm(onehot(column(1, c) == key_lane), bank[...])
        pick[c * LANES : (c + 1) * LANES, :] = jnp.where(
            column(2, c) == 0, rows[:, :LANES], rows[:, LANES:]
        ).astype(BF16)

    @pl.loop(0, 8)
    def _(q):
        slot = iota((256, LANES), 0) + q * 256
        sel = jnp.concatenate([onehot(place8[c : c + 1, :] == slot) for c in range(8)], axis=1)
        send[pl.ds(q * 16, 16)] = mm(sel, pick[...]).astype(BF16).reshape(16, CAP, LANES)

    edge_lo[0] = air_v[0:1, :]
    edge_hi[0] = air_v[15:16, :]
    field[:, LANES : LANES + 8192] = air_v[...]

    def pad_ends():
        field[:, :LANES] = jnp.broadcast_to(field[:, LANES : LANES + 1], (16, LANES))
        field[:, LANES + 8192 :] = jnp.broadcast_to(
            field[:, LANES + 8191 : LANES + 8192], (16, LANES)
        )

    pad_ends()

    pl.semaphore_wait(barrier, nspan + ngroup - 2)
    for peer in row_peers[1:]:
        pl.semaphore_signal(ready, inc=1, device_id=peer, device_id_type=MESH)

    def idx_row(j):
        g = (group + j) % ngroup
        return pltpu.make_async_remote_copy(
            idx_out.at[pl.ds(pl.multiple_of(g * nspan, nspan), nspan)],
            idx_row_in.at[group],
            send_sem.at[1], recv_sem.at[1],
            device_id=(span, g), device_id_type=MESH,
        )

    for j in range(1, ngroup):
        idx_row(j).start()
    idx_row_in[group] = idx_out[pl.ds(pl.multiple_of(group * nspan, nspan), nspan), :]

    def edges(step):
        east = ((span + 1) % nspan, group)
        west = ((span + nspan - 1) % nspan, group)
        return (
            pltpu.make_async_remote_copy(
                edge_hi.at[step], halo_w.at[step], edge_send.at[step, 0], edge_recv.at[step, 0],
                device_id=east, device_id_type=MESH,
            ),
            pltpu.make_async_remote_copy(
                edge_lo.at[step], halo_e.at[step], edge_send.at[step, 1], edge_recv.at[step, 1],
                device_id=west, device_id_type=MESH,
            ),
        )

    for e in edges(0):
        e.start()

    def scatter_all(src, dst, k):
        def to(s, g):
            pltpu.make_async_remote_copy(
                src.at[s * ngroup + g], dst.at[me], send_sem.at[k], recv_sem.at[k],
                device_id=(s, g), device_id_type=MESH,
            ).start()

        for s, g in row_peers[1:]:
            to(s, g)

        @pl.loop(1, nspan)
        def _(i):
            s = (span + i) % nspan
            for _, g in row_peers:
                to(s, g)

    def whole(src, dst, k):
        return pltpu.make_async_remote_copy(
            src.at[pl.ds(0, ndev - 1)], dst.at[pl.ds(0, ndev - 1)], send_sem.at[k], recv_sem.at[k],
            device_id=where_is((me + 1) % ndev), device_id_type=MESH,
        )

    pl.semaphore_wait(ready, ngroup - 1)
    scatter_all(send, recv, 0)
    recv[me] = send[me]
    both = pltpu.make_async_remote_copy(
        idx_row_in.at[pl.ds(0, ngroup - 1)], idx_row_in.at[pl.ds(0, ngroup - 1)],
        send_sem.at[1], recv_sem.at[1], device_id=row_peers[1], device_id_type=MESH,
    )
    both.wait_send()
    both.wait_recv()
    total = idx_row_in[0]
    for g in range(1, ngroup):
        total = total + idx_row_in[g]
    idx_mid[:, 0, :] = total

    def idx_column(i):
        s = (span + i) % nspan
        return pltpu.make_async_remote_copy(
            idx_mid.at[s], idx_in.at[span], send_sem.at[3], recv_sem.at[3],
            device_id=(s, group), device_id_type=MESH,
        )

    for i in range(1, nspan):
        idx_column(i).start()
    idx_in[span] = idx_mid[span]

    for c in range(8):
        slot_lane = iota((LANES, 2048), 1)
        pt_v[c * LANES : (c + 1) * LANES, :] = onehot(column(0, c) == slot_lane)

    @pl.loop(0, 8)
    def _(q):
        at = iota((LANES, LANES), 0) + q * LANES
        st_v[pl.ds(q * LANES, LANES), :] = jnp.concatenate(
            [onehot(key8[c : c + 1, :] == at) for c in range(8)], axis=1
        )

    loads[4].wait()
    nbr = (nbr_v[...] - (me - 1) * LANES).astype(F32)
    nbr8 = jnp.concatenate([nbr, nbr], axis=0)

    @pl.loop(0, 8)
    def _(q):
        tiled = jnp.concatenate([nbr8] * 16, axis=0)
        own_lane = (iota((LANES, LANES), 0) // 8 + q * 16) == iota((LANES, LANES), 1)
        link = jnp.sum(jnp.where(own_lane, tiled, F32(0.0)), axis=1, keepdims=True).astype(I32)
        near_map[pl.ds(q * LANES, LANES), :] = onehot(link == iota((LANES, 3 * LANES), 1))

    loads[6].wait()
    loads[7].wait()

    def advance(step):
        for e in edges(step):
            e.wait()
        wide = 1024
        row = iota((16, wide), 0)
        fresh = []
        for j in range(8192 // wide):
            ext = field[:, j * wide : j * wide + wide + 2 * LANES]
            t = ext[:, LANES : LANES + wide]
            north = pltpu.roll(ext, wide + 2 * LANES - 1, 1)[:, LANES : LANES + wide]
            south = pltpu.roll(ext, 1, 1)[:, LANES : LANES + wide]
            cut = slice(j * wide, (j + 1) * wide)
            east = jnp.where(row == 15, halo_e[step, :, cut], pltpu.roll(t, 15, 0))
            west = jnp.where(row == 0, halo_w[step, :, cut], pltpu.roll(t, 1, 0))
            new = (
                t
                + kap_v[:, cut] * ((east + west) + (north + south) - 4.0 * t)
                - (0.5 * vel_v[:, cut]) * (east - west)
            )
            new = jnp.where(iota((16, wide), 1) + j * wide < width, new, t)
            air_v[:, cut] = new
        field[:, LANES : LANES + 8192] = air_v[...]
        if step + 1 < STEPS:
            pad_ends()
            edge_lo[step + 1] = air_v[0:1, :]
            edge_hi[step + 1] = air_v[15:16, :]
            for e in edges(step + 1):
                e.start()

    advance(0)

    loads[5].wait()
    sub = jnp.concatenate([sub_v[...], sub_v[...]], axis=0).T
    both = pltpu.make_async_remote_copy(
        idx_mid.at[pl.ds(0, nspan - 1)], idx_in.at[pl.ds(0, nspan - 1)],
        send_sem.at[3], recv_sem.at[3], device_id=column_peers[1], device_id_type=MESH,
    )
    both.wait_send()
    both.wait_recv()
    for q in range(16):
        at = idx_in[q].astype(I32)
        t_q = jnp.where(at == iota((LANES, LANES), 0) + 1, F32(1.0), F32(0.0))
        t_v[:, q * LANES : (q + 1) * LANES] = t_q.astype(BF16)
        tt_v[q * LANES : (q + 1) * LANES, :] = t_q.T.astype(BF16)
    hits_b = mm(t_v[...], jnp.ones((2048, LANES), BF16))
    both = whole(send, recv, 0)
    both.wait_send()
    both.wait_recv()
    total = mm(t_v[...], recv[...].reshape(2048, LANES))
    total = total + pltpu.roll(total, 64, 1)
    sub = sub + UPTAKE * (total - hits_b * sub)

    def sides(step):
        nxt = where_is((me + 1) % ndev)
        prev = where_is((me + ndev - 1) % ndev)
        return (
            pltpu.make_async_remote_copy(
                beside.at[step, 1], beside.at[step, 0], side_send.at[step, 0], side_recv.at[step, 0],
                device_id=nxt, device_id_type=MESH,
            ),
            pltpu.make_async_remote_copy(
                beside.at[step, 1], beside.at[step, 2], side_send.at[step, 1], side_recv.at[step, 1],
                device_id=prev, device_id_type=MESH,
            ),
        )

    lane2 = iota((LANES, LANES), 1)
    row2 = iota((LANES, LANES), 0)
    gather_i = onehot((lane2 % 64) // 2 == row2 // 4)
    gather_i = jnp.concatenate([gather_i, gather_i], axis=0)
    per_block = onehot(iota((LANES, 8 * LANES), 1) // 8 == iota((LANES, 8 * LANES), 0))
    half_lane = (iota((8 * LANES, LANES), 0) % 8) // 4 == iota((8 * LANES, LANES), 1) // 64
    even_block = iota((8 * LANES, LANES), 0) // 8 % 2 == 0
    odd_lane = (iota((8 * LANES, LANES), 0) % 8) // 4 == iota((8 * LANES, LANES), 1) % 2
    same = iota((16, LANES), 0) % 4 == iota((16, LANES), 1) % 4

    for step in range(SSTEPS):
        beside[step, 1] = sub.astype(BF16)
        for s in sides(step):
            s.start()
        advance(step + 1)
        if step == 0:
            loads[8].wait()
        for s in sides(step):
            s.wait()
        near = mm(near_map[...], beside[step].reshape(3 * LANES, LANES))
        near = jnp.where(half_lane, near, F32(0.0))
        near_v[:, :LANES] = jnp.where(even_block, near, F32(0.0)).astype(BF16)
        near_v[:, LANES:] = jnp.where(even_block, F32(0.0), near).astype(BF16)

        @pl.loop(0, 32, unroll=32)
        def _(p):
            quad = [c_v[pl.ds(p * 512 + b * LANES, LANES), :] for b in range(4)]
            pairs = jnp.concatenate(
                [
                    jnp.concatenate(quad[:2], axis=1),
                    jnp.concatenate(quad[2:], axis=1),
                ],
                axis=0,
            )
            res = mm_nt(near_v[pl.ds(p * 32, 32), :], pairs)
            z_v[pl.ds(p * 32, 16), :LANES] = jnp.where(same, res[:16, :LANES], F32(0.0))
            z_v[pl.ds(p * 32 + 16, 16), :LANES] = jnp.where(same, res[16:, LANES:], F32(0.0))

        hi, lo = split(z_v[:, :LANES])
        w = mm(jnp.concatenate([hi, lo], axis=1), gather_i)
        hi, lo = split(jnp.where(odd_lane, w, F32(0.0)))
        added = mm(per_block, jnp.concatenate([hi, lo], axis=1))
        sub = sub + (added[:, :LANES] + added[:, LANES:])

    hi = sub.astype(BF16).astype(F32)
    pair = jnp.where(lane2 < 64, hi, sub - hi).astype(BF16)
    back[...] = mm(tt_v[...], pair).astype(BF16).reshape(ndev, CAP, LANES)
    scatter_all(back, got, 2)
    got[me] = back[me]
    sub_o[...] = sub.T[:64, :]
    advance(3)
    both = whole(back, got, 2)
    both.wait_send()
    both.wait_recv()

    for c in range(8):
        rows = slice(c * LANES, (c + 1) * LANES)
        surf = mm(pt_v[rows, :], got[...].reshape(2048, LANES))
        gap = surf - pick[rows, :].astype(F32)
        gap = RELEASE * (gap + pltpu.roll(gap, 64, 1))
        keep = jnp.logical_and(column(5, c) == 1, column(2, c) == lane2 // 64)
        hi, lo = split(jnp.where(keep, gap, F32(0.0)))
        bank[rows, :LANES] = hi
        bank[rows, LANES:] = lo
    z_v[...] = mm(st_v[...], bank[...])
    for line in range(2):
        for j in range(64):
            k = (line * 64 + j) * 8
            cut = slice(j * LANES, (j + 1) * LANES)
            air_o[line * 8 : line * 8 + 8, cut] = air_v[line * 8 : line * 8 + 8, cut] + (
                z_v[k : k + 8, :LANES] + z_v[k : k + 8, LANES:]
            )


def per_device(
    nspan,
    ngroup,
    air_temp,
    air_vel,
    air_kappa,
    group_width,
    sub_temp,
    sub_coupling,
    neighbors,
    iface_count,
    iface_seg,
    iface_owner,
    iface_block,
):
    cells, section = air_temp.shape[1:]
    blocks, links, _ = sub_coupling.shape
    coupling = (
        sub_coupling.reshape(blocks, links, 32, LANES)
        .transpose(0, 2, 1, 3)
        .reshape(blocks * links * 32, LANES)
    )
    ndev = nspan * ngroup
    vmem = pltpu.VMEM
    dma = pltpu.SemaphoreType.DMA
    any_space = pl.BlockSpec(memory_space=pl.ANY)
    smem = pl.BlockSpec(memory_space=pltpu.SMEM)
    in_vmem = pl.BlockSpec(memory_space=pltpu.VMEM)
    air, sub = pl.pallas_call(
        functools.partial(kernel, nspan, ngroup),
        out_shape=(
            jax.ShapeDtypeStruct((cells, section), F32),
            jax.ShapeDtypeStruct((NODES, blocks), F32),
        ),
        in_specs=[any_space] * 3 + [smem] + [any_space] * 3 + [smem] + [any_space] * 3,
        out_specs=(in_vmem, in_vmem),
        scratch_shapes=[
            vmem((cells, section), F32),
            vmem((cells, section), F32),
            vmem((cells, section), F32),
            vmem((NODES, blocks), F32),
            vmem(coupling.shape, BF16),
            vmem((links, blocks), I32),
            vmem((8, LANES), I32),
            vmem((8, LANES), I32),
            vmem((8, LANES), I32),
            vmem((cells, section + 2 * LANES), F32),
            vmem((8 * LANES, 2 * LANES), BF16),
            vmem((8 * LANES, LANES), BF16),
            vmem((ndev, CAP, LANES), BF16),
            vmem((ndev, CAP, LANES), BF16),
            vmem((ndev, CAP, LANES), BF16),
            vmem((ndev, CAP, LANES), BF16),
            vmem((ndev, LANES), F32),
            vmem((ngroup, nspan, LANES), F32),
            vmem((nspan, 1, LANES), F32),
            vmem((nspan, 1, LANES), F32),
            vmem((LANES, ndev * CAP), BF16),
            vmem((ndev * CAP, LANES), BF16),
            vmem((8 * LANES, ndev * CAP), BF16),
            vmem((8 * LANES, 8 * LANES), BF16),
            vmem((8 * LANES, 3 * LANES), BF16),
            vmem((8 * LANES, 2 * LANES), BF16),
            vmem((8 * LANES, 2 * LANES), F32),
            vmem((SSTEPS, 3, LANES, LANES), BF16),
            vmem((STEPS, 1, section), F32),
            vmem((STEPS, 1, section), F32),
            vmem((STEPS, 1, section), F32),
            vmem((STEPS, 1, section), F32),
            dma((9,)),
            dma((4,)),
            dma((4,)),
            dma((STEPS, 2)),
            dma((STEPS, 2)),
            dma((SSTEPS, 2)),
            dma((SSTEPS, 2)),
            pltpu.SemaphoreType.REGULAR,
        ],
        compiler_params=pltpu.CompilerParams(
            collective_id=0, has_side_effects=True, vmem_limit_bytes=28 << 20
        ),
    )(
        pltpu.with_memory_space_constraint(air_temp.reshape(cells, section), pltpu.HBM),
        pltpu.with_memory_space_constraint(air_vel.reshape(cells, section), pltpu.HBM),
        pltpu.with_memory_space_constraint(air_kappa.reshape(cells, section), pltpu.HBM),
        group_width,
        pltpu.with_memory_space_constraint(sub_temp.T, pltpu.HBM),
        pltpu.with_memory_space_constraint(coupling, pltpu.HBM),
        pltpu.with_memory_space_constraint(neighbors.T, pltpu.HBM),
        iface_count,
        pltpu.with_memory_space_constraint(iface_seg.reshape(8, LANES), pltpu.HBM),
        pltpu.with_memory_space_constraint(iface_owner.reshape(8, LANES), pltpu.HBM),
        pltpu.with_memory_space_constraint(iface_block.reshape(8, LANES), pltpu.HBM),
    )
    return air.reshape(1, cells, section), sub.T


def solution(mesh):
    placed = (
        P("group", "span", None),
        P("group", "span", None),
        P("group", "span", None),
        P("group"),
        P(("span", "group"), None),
        P(("span", "group"), None, None),
        P(("span", "group"), None),
        P(("span", "group")),
        P(("span", "group")),
        P(("span", "group"), None),
        P(("span", "group")),
    )
    return jax.shard_map(
        functools.partial(per_device, mesh.shape["span"], mesh.shape["group"]),
        mesh=mesh,
        in_specs=placed,
        out_specs=(P("group", "span", None), P(("span", "group"), None)),
        check_vma=False,
    )
```

```python
import functools

import jax
import jax.numpy as jnp
from jax import lax
from jax.experimental import pallas as pl
from jax.experimental.pallas import tpu as pltpu
from jax.sharding import PartitionSpec as P

STEPS = 4
SSTEPS = 2
NODES = 64
CAP = 16
LANES = 128
UPTAKE = 0.3
RELEASE = 0.5
MESH = pl.DeviceIdType.MESH
F32 = jnp.float32
BF16 = jnp.bfloat16
I32 = jnp.int32


def iota(shape, dim):
    return lax.broadcasted_iota(I32, shape, dim)


def onehot(mask):
    return jnp.where(mask, F32(1.0), F32(0.0)).astype(BF16)


def mm(a, b):
    return jnp.dot(a, b, preferred_element_type=F32)


def mm_nt(a, b):
    return lax.dot_general(a, b, (((1,), (1,)), ((), ())), preferred_element_type=F32)


def split(x):
    hi = x.astype(BF16)
    lo = (x - hi.astype(F32)).astype(BF16)
    return hi, lo


def kernel(
    nspan,
    ngroup,
    air_h,
    vel_h,
    kap_h,
    width_s,
    sub_h,
    c_h,
    nbr_h,
    count_s,
    seg_h,
    own_h,
    blk_h,
    air_o,
    sub_o,
    air_v,
    vel_v,
    kap_v,
    sub_v,
    c_v,
    nbr_v,
    seg_v,
    own_v,
    blk_v,
    field,
    bank,
    pick,
    pick2,
    send,
    recv,
    back,
    got,
    idx_out,
    idx_row_in,
    idx_mid,
    idx_in,
    t_v,
    tt_v,
    pt_v,
    st_v,
    near_map,
    near_v,
    z_v,
    beside,
    edge_lo,
    edge_hi,
    halo_w,
    halo_e,
    in_sem,
    send_sem,
    recv_sem,
    edge_send,
    edge_recv,
    side_send,
    side_recv,
    ready,
):
    ndev = nspan * ngroup
    span = lax.axis_index("span")
    group = lax.axis_index("group")
    me = span * ngroup + group

    def where_is(d):
        return (d // ngroup, d % ngroup)

    loads = []
    for k, (src, dst) in enumerate(
        (
            (own_h, own_v),
            (seg_h, seg_v),
            (blk_h, blk_v),
            (air_h, air_v),
            (nbr_h, nbr_v),
            (sub_h, sub_v),
            (vel_h, vel_v),
            (kap_h, kap_v),
            (c_h, c_v),
        )
    ):
        copy = pltpu.make_async_copy(src, dst, in_sem.at[k])
        copy.start()
        loads.append(copy)

    barrier = pltpu.get_barrier_semaphore()

    row_peers = [(span, (group + j) % ngroup) for j in range(ngroup)]
    column_peers = [((span + i) % nspan, group) for i in range(nspan)]
    for peer in row_peers[1:] + column_peers[1:]:
        pl.semaphore_signal(barrier, inc=1, device_id=peer, device_id_type=MESH)

    count = count_s[0]
    width = width_s[0]
    lane = iota((1, LANES), 1)

    for k in range(3):
        loads[k].wait()
    own8 = own_v[...]
    seg8 = seg_v[...]
    blk8 = blk_v[...]
    active8 = (iota((8, LANES), 0) * LANES + iota((8, LANES), 1)) < count
    sub128 = iota((LANES, LANES), 0)
    hits = [own8[c : c + 1, :] == sub128 for c in range(8)]
    upper = onehot(iota((LANES, 2 * LANES), 0) < iota((LANES, 2 * LANES), 1))
    ahead = mm(jnp.concatenate([onehot(h) for h in hits], axis=0), upper)
    carry = jnp.zeros((LANES, LANES), F32)
    ranks = []
    for c in range(8):
        part = ahead[c * LANES : (c + 1) * LANES]
        ranks.append(
            jnp.sum(jnp.where(hits[c], part[:, :LANES] + carry, F32(0.0)), axis=0, keepdims=True)
        )
        carry = carry + part[:, LANES:]
    rank8 = jnp.concatenate(ranks, axis=0)
    place8 = jnp.where(active8, own8 * CAP + rank8.astype(I32), -1)
    line8 = seg8 // LANES
    key8 = (line8 // 8) * 512 + ((seg8 % LANES) // 2) * 8 + line8 % 8
    half8 = seg8 % 2
    shift8 = jnp.where(active8, rank8.astype(I32) + group * CAP, -1)
    table = jnp.concatenate(
        [
            jnp.where(active8, place8 % 1024, -1).astype(F32),
            key8.astype(F32),
            half8.astype(F32),
            shift8.astype(F32),
            (blk8 + 1).astype(F32),
            active8.astype(F32),
            (place8 // 1024).astype(F32),
            jnp.zeros((LANES - 56, LANES), F32),
        ],
        axis=0,
    )
    columns = table.T.astype(I32)

    def column(a, c):
        return columns[:, a * 8 + c : a * 8 + c + 1]

    slots = jnp.concatenate(
        [
            jnp.where(column(3, c) == lane, column(4, c).astype(F32), F32(0.0)).astype(BF16)
            for c in range(8)
        ],
        axis=0,
    )
    spot8 = (own8 % ngroup) * nspan + own8 // ngroup
    owners = jnp.concatenate([onehot(spot8[c : c + 1, :] == sub128) for c in range(8)], axis=1)
    idx_out[...] = mm(owners, slots)

    loads[3].wait()
    for line in range(2):
        for j in range(64):
            k = (line * 64 + j) * 8
            a = air_v[line * 8 : line * 8 + 8, j * LANES : (j + 1) * LANES]
            hi = a.astype(BF16).astype(F32)
            lo = a - hi
            z_v[k : k + 8, :LANES] = jnp.where(lane < 64, hi, pltpu.roll(lo, 64, 1))
            z_v[k : k + 8, LANES:] = jnp.where(lane < 64, pltpu.roll(hi, 64, 1), lo)
    bank[...] = z_v[...].astype(BF16)
    pl.semaphore_wait(barrier, nspan + ngroup - 2)
    for peer in row_peers[1:]:
        pl.semaphore_signal(ready, inc=1, device_id=peer, device_id_type=MESH)

    def idx_row(j):
        g = (group + j) % ngroup
        return pltpu.make_async_remote_copy(
            idx_out.at[pl.ds(pl.multiple_of(g * nspan, nspan), nspan)],
            idx_row_in.at[group],
            send_sem.at[1], recv_sem.at[1],
            device_id=(span, g), device_id_type=MESH,
        )

    for j in range(1, ngroup):
        idx_row(j).start()
    idx_row_in[group] = idx_out[pl.ds(pl.multiple_of(group * nspan, nspan), nspan), :]

    key_lane = iota((LANES, 8 * LANES), 1)
    for c in range(8):
        rows = mm(onehot(column(1, c) == key_lane), bank[...])
        rows = jnp.where(column(2, c) == 0, rows[:, :LANES], rows[:, LANES:])
        cut = slice(c * LANES, (c + 1) * LANES)
        pick[cut, :] = rows.astype(BF16)
        pick2[cut, :LANES] = jnp.where(column(6, c) == 0, rows, F32(0.0)).astype(BF16)
        pick2[cut, LANES:] = jnp.where(column(6, c) == 1, rows, F32(0.0)).astype(BF16)

    def send_rows(src, dst, k, s, skip_self):
        for n, (_, g) in enumerate(row_peers):
            copy = pltpu.make_async_remote_copy(
                src.at[s * ngroup + g], dst.at[me], send_sem.at[k], recv_sem.at[k],
                device_id=(s, g), device_id_type=MESH,
            )
            if n == 0:
                pl.when(skip_self)(copy.start)
            else:
                copy.start()

    place8m = jnp.where(active8, place8 % 1024, -1)
    pl.semaphore_wait(ready, ngroup - 1)

    def pack_and_send(i):
        u = (span + i) % 8
        slot = iota((LANES, LANES), 0) + u * LANES
        sel = jnp.concatenate([onehot(place8m[c : c + 1, :] == slot) for c in range(8)], axis=1)
        rows = mm(sel, pick2[...]).astype(BF16)
        send[pl.ds(u * ngroup, ngroup)] = rows[:, :LANES].reshape(ngroup, CAP, LANES)
        send[pl.ds((u + 8) * ngroup, ngroup)] = rows[:, LANES:].reshape(ngroup, CAP, LANES)
        for a in range(2):
            s = (span + i + 8 * a) % nspan
            send_rows(send, recv, 0, s, s != span)

    pl.loop(0, 4)(pack_and_send)
    both = pltpu.make_async_remote_copy(
        idx_row_in.at[pl.ds(0, ngroup - 1)], idx_row_in.at[pl.ds(0, ngroup - 1)],
        send_sem.at[1], recv_sem.at[1], device_id=row_peers[1], device_id_type=MESH,
    )
    both.wait_send()
    both.wait_recv()
    total = idx_row_in[0]
    for g in range(1, ngroup):
        total = total + idx_row_in[g]
    idx_mid[:, 0, :] = total

    def idx_column(i):
        s = (span + i) % nspan
        return pltpu.make_async_remote_copy(
            idx_mid.at[s], idx_in.at[span], send_sem.at[3], recv_sem.at[3],
            device_id=(s, group), device_id_type=MESH,
        )

    for i in range(1, nspan):
        idx_column(i).start()
    idx_in[span] = idx_mid[span]

    pl.loop(4, 8)(pack_and_send)

    edge_lo[0] = air_v[0:1, :]
    edge_hi[0] = air_v[15:16, :]
    field[:, LANES : LANES + 8192] = air_v[...]

    def pad_ends():
        field[:, :LANES] = jnp.broadcast_to(field[:, LANES : LANES + 1], (16, LANES))
        field[:, LANES + 8192 :] = jnp.broadcast_to(
            field[:, LANES + 8191 : LANES + 8192], (16, LANES)
        )

    pad_ends()

    def edges(step):
        east = ((span + 1) % nspan, group)
        west = ((span + nspan - 1) % nspan, group)
        return (
            pltpu.make_async_remote_copy(
                edge_hi.at[step], halo_w.at[step], edge_send.at[step, 0], edge_recv.at[step, 0],
                device_id=east, device_id_type=MESH,
            ),
            pltpu.make_async_remote_copy(
                edge_lo.at[step], halo_e.at[step], edge_send.at[step, 1], edge_recv.at[step, 1],
                device_id=west, device_id_type=MESH,
            ),
        )

    for e in edges(0):
        e.start()

    def whole(src, dst, k):
        return pltpu.make_async_remote_copy(
            src.at[pl.ds(0, ndev - 1)], dst.at[pl.ds(0, ndev - 1)], send_sem.at[k], recv_sem.at[k],
            device_id=where_is((me + 1) % ndev), device_id_type=MESH,
        )

    recv[me] = send[me]
    for c in range(8):
        slot_lane = iota((LANES, 1024), 1)
        pt_v[c * LANES : (c + 1) * LANES, :] = onehot(column(0, c) == slot_lane)

    @pl.loop(0, 8)
    def _(q):
        at = iota((LANES, LANES), 0) + q * LANES
        st_v[pl.ds(q * LANES, LANES), :] = jnp.concatenate(
            [onehot(key8[c : c + 1, :] == at) for c in range(8)], axis=1
        )

    loads[4].wait()
    nbr = (nbr_v[...] - (me - 1) * LANES).astype(F32)
    nbr8 = jnp.concatenate([nbr, nbr], axis=0)

    @pl.loop(0, 8)
    def _(q):
        tiled = jnp.concatenate([nbr8] * 16, axis=0)
        own_lane = (iota((LANES, LANES), 0) // 8 + q * 16) == iota((LANES, LANES), 1)
        link = jnp.sum(jnp.where(own_lane, tiled, F32(0.0)), axis=1, keepdims=True).astype(I32)
        near_map[pl.ds(q * LANES, LANES), :] = onehot(link == iota((LANES, 3 * LANES), 1))

    loads[6].wait()
    loads[7].wait()

    def advance(step):
        for e in edges(step):
            e.wait()
        wide = 1024
        row = iota((16, wide), 0)
        fresh = []
        for j in range(8192 // wide):
            ext = field[:, j * wide : j * wide + wide + 2 * LANES]
            t = ext[:, LANES : LANES + wide]
            north = pltpu.roll(ext, wide + 2 * LANES - 1, 1)[:, LANES : LANES + wide]
            south = pltpu.roll(ext, 1, 1)[:, LANES : LANES + wide]
            cut = slice(j * wide, (j + 1) * wide)
            east = jnp.where(row == 15, halo_e[step, :, cut], pltpu.roll(t, 15, 0))
            west = jnp.where(row == 0, halo_w[step, :, cut], pltpu.roll(t, 1, 0))
            new = (
                t
                + kap_v[:, cut] * ((east + west) + (north + south) - 4.0 * t)
                - (0.5 * vel_v[:, cut]) * (east - west)
            )
            new = jnp.where(iota((16, wide), 1) + j * wide < width, new, t)
            air_v[:, cut] = new
        field[:, LANES : LANES + 8192] = air_v[...]
        if step + 1 < STEPS:
            pad_ends()
            edge_lo[step + 1] = air_v[0:1, :]
            edge_hi[step + 1] = air_v[15:16, :]
            for e in edges(step + 1):
                e.start()

    advance(0)

    loads[5].wait()
    sub = jnp.concatenate([sub_v[...], sub_v[...]], axis=0).T
    both = pltpu.make_async_remote_copy(
        idx_mid.at[pl.ds(0, nspan - 1)], idx_in.at[pl.ds(0, nspan - 1)],
        send_sem.at[3], recv_sem.at[3], device_id=column_peers[1], device_id_type=MESH,
    )
    both.wait_send()
    both.wait_recv()
    for q in range(16):
        at = idx_in[q].astype(I32)
        t_q = jnp.where(at == iota((LANES, LANES), 0) + 1, F32(1.0), F32(0.0))
        t_v[:, q * LANES : (q + 1) * LANES] = t_q.astype(BF16)
        tt_v[q * LANES : (q + 1) * LANES, :] = t_q.T.astype(BF16)
    hits_b = mm(t_v[...], jnp.ones((2048, LANES), BF16))
    both = whole(send, recv, 0)
    both.wait_send()
    both.wait_recv()
    total = mm(t_v[...], recv[...].reshape(2048, LANES))
    total = total + pltpu.roll(total, 64, 1)
    sub = sub + UPTAKE * (total - hits_b * sub)

    def sides(step):
        nxt = where_is((me + 1) % ndev)
        prev = where_is((me + ndev - 1) % ndev)
        return (
            pltpu.make_async_remote_copy(
                beside.at[step, 1], beside.at[step, 0], side_send.at[step, 0], side_recv.at[step, 0],
                device_id=nxt, device_id_type=MESH,
            ),
            pltpu.make_async_remote_copy(
                beside.at[step, 1], beside.at[step, 2], side_send.at[step, 1], side_recv.at[step, 1],
                device_id=prev, device_id_type=MESH,
            ),
        )

    lane2 = iota((LANES, LANES), 1)
    row2 = iota((LANES, LANES), 0)
    gather_i = onehot((lane2 % 64) // 2 == row2 // 4)
    gather_i = jnp.concatenate([gather_i, gather_i], axis=0)
    per_block = onehot(iota((LANES, 8 * LANES), 1) // 8 == iota((LANES, 8 * LANES), 0))
    half_lane = (iota((8 * LANES, LANES), 0) % 8) // 4 == iota((8 * LANES, LANES), 1) // 64
    even_block = iota((8 * LANES, LANES), 0) // 8 % 2 == 0
    odd_lane = (iota((8 * LANES, LANES), 0) % 8) // 4 == iota((8 * LANES, LANES), 1) % 2
    same = iota((16, LANES), 0) % 4 == iota((16, LANES), 1) % 4

    for step in range(SSTEPS):
        beside[step, 1] = sub.astype(BF16)
        for s in sides(step):
            s.start()
        advance(step + 1)
        if step == 0:
            loads[8].wait()
        for s in sides(step):
            s.wait()
        near = mm(near_map[...], beside[step].reshape(3 * LANES, LANES))
        near = jnp.where(half_lane, near, F32(0.0))
        near_v[:, :LANES] = jnp.where(even_block, near, F32(0.0)).astype(BF16)
        near_v[:, LANES:] = jnp.where(even_block, F32(0.0), near).astype(BF16)

        @pl.loop(0, 32, unroll=32)
        def _(p):
            quad = [c_v[pl.ds(p * 512 + b * LANES, LANES), :] for b in range(4)]
            pairs = jnp.concatenate(
                [
                    jnp.concatenate(quad[:2], axis=1),
                    jnp.concatenate(quad[2:], axis=1),
                ],
                axis=0,
            )
            res = mm_nt(near_v[pl.ds(p * 32, 32), :], pairs)
            z_v[pl.ds(p * 32, 16), :LANES] = jnp.where(same, res[:16, :LANES], F32(0.0))
            z_v[pl.ds(p * 32 + 16, 16), :LANES] = jnp.where(same, res[16:, LANES:], F32(0.0))

        hi, lo = split(z_v[:, :LANES])
        w = mm(jnp.concatenate([hi, lo], axis=1), gather_i)
        hi, lo = split(jnp.where(odd_lane, w, F32(0.0)))
        added = mm(per_block, jnp.concatenate([hi, lo], axis=1))
        sub = sub + (added[:, :LANES] + added[:, LANES:])

    hi = sub.astype(BF16).astype(F32)
    pair = jnp.where(lane2 < 64, hi, sub - hi).astype(BF16)
    @pl.loop(0, 8)
    def _(i):
        q = (span // 2 + i) % 8
        rows = mm(tt_v[pl.ds(q * 256, 256), :], pair)
        back[pl.ds(q * 16, 16)] = rows.astype(BF16).reshape(16, CAP, LANES)
        for a in range(2):
            s = q * 2 + (span + a) % 2
            send_rows(back, got, 2, s, s != span)

    got[me] = back[me]
    sub_o[...] = sub.T[:64, :]
    advance(3)
    both = whole(back, got, 2)
    both.wait_send()
    both.wait_recv()

    got2 = jnp.concatenate(
        [got[:64].reshape(1024, LANES), got[64:].reshape(1024, LANES)], axis=1
    )
    for c in range(8):
        rows = slice(c * LANES, (c + 1) * LANES)
        surf = mm(pt_v[rows, :], got2)
        surf = jnp.where(column(6, c) == 0, surf[:, :LANES], surf[:, LANES:])
        gap = surf - pick[rows, :].astype(F32)
        gap = RELEASE * (gap + pltpu.roll(gap, 64, 1))
        keep = jnp.logical_and(column(5, c) == 1, column(2, c) == lane2 // 64)
        hi, lo = split(jnp.where(keep, gap, F32(0.0)))
        bank[rows, :LANES] = hi
        bank[rows, LANES:] = lo
    z_v[...] = mm(st_v[...], bank[...])
    for line in range(2):
        for j in range(64):
            k = (line * 64 + j) * 8
            cut = slice(j * LANES, (j + 1) * LANES)
            air_o[line * 8 : line * 8 + 8, cut] = air_v[line * 8 : line * 8 + 8, cut] + (
                z_v[k : k + 8, :LANES] + z_v[k : k + 8, LANES:]
            )


def per_device(
    nspan,
    ngroup,
    air_temp,
    air_vel,
    air_kappa,
    group_width,
    sub_temp,
    sub_coupling,
    neighbors,
    iface_count,
    iface_seg,
    iface_owner,
    iface_block,
):
    cells, section = air_temp.shape[1:]
    blocks, links, _ = sub_coupling.shape
    coupling = (
        sub_coupling.reshape(blocks, links, 32, LANES)
        .transpose(0, 2, 1, 3)
        .reshape(blocks * links * 32, LANES)
    )
    ndev = nspan * ngroup
    vmem = pltpu.VMEM
    dma = pltpu.SemaphoreType.DMA
    any_space = pl.BlockSpec(memory_space=pl.ANY)
    smem = pl.BlockSpec(memory_space=pltpu.SMEM)
    in_vmem = pl.BlockSpec(memory_space=pltpu.VMEM)
    air, sub = pl.pallas_call(
        functools.partial(kernel, nspan, ngroup),
        out_shape=(
            jax.ShapeDtypeStruct((cells, section), F32),
            jax.ShapeDtypeStruct((NODES, blocks), F32),
        ),
        in_specs=[any_space] * 3 + [smem] + [any_space] * 3 + [smem] + [any_space] * 3,
        out_specs=(in_vmem, in_vmem),
        scratch_shapes=[
            vmem((cells, section), F32),
            vmem((cells, section), F32),
            vmem((cells, section), F32),
            vmem((NODES, blocks), F32),
            vmem(coupling.shape, BF16),
            vmem((links, blocks), I32),
            vmem((8, LANES), I32),
            vmem((8, LANES), I32),
            vmem((8, LANES), I32),
            vmem((cells, section + 2 * LANES), F32),
            vmem((8 * LANES, 2 * LANES), BF16),
            vmem((8 * LANES, LANES), BF16),
            vmem((8 * LANES, 2 * LANES), BF16),
            vmem((ndev, CAP, LANES), BF16),
            vmem((ndev, CAP, LANES), BF16),
            vmem((ndev, CAP, LANES), BF16),
            vmem((ndev, CAP, LANES), BF16),
            vmem((ndev, LANES), F32),
            vmem((ngroup, nspan, LANES), F32),
            vmem((nspan, 1, LANES), F32),
            vmem((nspan, 1, LANES), F32),
            vmem((LANES, ndev * CAP), BF16),
            vmem((ndev * CAP, LANES), BF16),
            vmem((8 * LANES, ndev * CAP // 2), BF16),
            vmem((8 * LANES, 8 * LANES), BF16),
            vmem((8 * LANES, 3 * LANES), BF16),
            vmem((8 * LANES, 2 * LANES), BF16),
            vmem((8 * LANES, 2 * LANES), F32),
            vmem((SSTEPS, 3, LANES, LANES), BF16),
            vmem((STEPS, 1, section), F32),
            vmem((STEPS, 1, section), F32),
            vmem((STEPS, 1, section), F32),
            vmem((STEPS, 1, section), F32),
            dma((9,)),
            dma((4,)),
            dma((4,)),
            dma((STEPS, 2)),
            dma((STEPS, 2)),
            dma((SSTEPS, 2)),
            dma((SSTEPS, 2)),
            pltpu.SemaphoreType.REGULAR,
        ],
        compiler_params=pltpu.CompilerParams(
            collective_id=0, has_side_effects=True, vmem_limit_bytes=28 << 20
        ),
    )(
        pltpu.with_memory_space_constraint(air_temp.reshape(cells, section), pltpu.HBM),
        pltpu.with_memory_space_constraint(air_vel.reshape(cells, section), pltpu.HBM),
        pltpu.with_memory_space_constraint(air_kappa.reshape(cells, section), pltpu.HBM),
        group_width,
        pltpu.with_memory_space_constraint(sub_temp.T, pltpu.HBM),
        pltpu.with_memory_space_constraint(coupling, pltpu.HBM),
        pltpu.with_memory_space_constraint(neighbors.T, pltpu.HBM),
        iface_count,
        pltpu.with_memory_space_constraint(iface_seg.reshape(8, LANES), pltpu.HBM),
        pltpu.with_memory_space_constraint(iface_owner.reshape(8, LANES), pltpu.HBM),
        pltpu.with_memory_space_constraint(iface_block.reshape(8, LANES), pltpu.HBM),
    )
    return air.reshape(1, cells, section), sub.T


def solution(mesh):
    placed = (
        P("group", "span", None),
        P("group", "span", None),
        P("group", "span", None),
        P("group"),
        P(("span", "group"), None),
        P(("span", "group"), None, None),
        P(("span", "group"), None),
        P(("span", "group")),
        P(("span", "group")),
        P(("span", "group"), None),
        P(("span", "group")),
    )
    return jax.shard_map(
        functools.partial(per_device, mesh.shape["span"], mesh.shape["group"]),
        mesh=mesh,
        in_specs=placed,
        out_specs=(P("group", "span", None), P(("span", "group"), None)),
        check_vma=False,
    )
```

```python
import functools

import jax
import jax.numpy as jnp
from jax import lax
from jax.experimental import pallas as pl
from jax.experimental.pallas import tpu as pltpu
from jax.sharding import PartitionSpec as P

STEPS = 4
SSTEPS = 2
NODES = 64
CAP = 16
LANES = 128
UPTAKE = 0.3
RELEASE = 0.5
MESH = pl.DeviceIdType.MESH
F32 = jnp.float32
BF16 = jnp.bfloat16
I32 = jnp.int32


def iota(shape, dim):
    return lax.broadcasted_iota(I32, shape, dim)


def onehot(mask):
    return jnp.where(mask, F32(1.0), F32(0.0)).astype(BF16)


def mm(a, b):
    return jnp.dot(a, b, preferred_element_type=F32)


def mm_nt(a, b):
    return lax.dot_general(a, b, (((1,), (1,)), ((), ())), preferred_element_type=F32)


def split(x):
    hi = x.astype(BF16)
    lo = (x - hi.astype(F32)).astype(BF16)
    return hi, lo


def kernel(
    nspan,
    ngroup,
    air_h,
    vel_h,
    kap_h,
    width_s,
    sub_h,
    c_h,
    nbr_h,
    count_s,
    seg_h,
    own_h,
    blk_h,
    air_o,
    sub_o,
    air_v,
    vel_v,
    kap_v,
    sub_v,
    c_v,
    nbr_v,
    seg_v,
    own_v,
    blk_v,
    field,
    bank,
    pick,
    pick2,
    send,
    recv,
    back,
    got,
    idx_out,
    idx_row_in,
    idx_mid,
    idx_in,
    t_v,
    tt_v,
    pt_v,
    st_v,
    near_map,
    near_v,
    z_v,
    beside,
    edge_lo,
    edge_hi,
    halo_w,
    halo_e,
    in_sem,
    send_sem,
    recv_sem,
    edge_send,
    edge_recv,
    side_send,
    side_recv,
    ready,
):
    ndev = nspan * ngroup
    span = lax.axis_index("span")
    group = lax.axis_index("group")
    me = span * ngroup + group

    def where_is(d):
        return (d // ngroup, d % ngroup)

    loads = []
    for k, (src, dst) in enumerate(
        (
            (own_h, own_v),
            (seg_h, seg_v),
            (blk_h, blk_v),
            (air_h, air_v),
            (nbr_h, nbr_v),
            (sub_h, sub_v),
            (vel_h, vel_v),
            (kap_h, kap_v),
            (c_h, c_v),
        )
    ):
        copy = pltpu.make_async_copy(src, dst, in_sem.at[k])
        if k < 6:
            copy.start()
        loads.append(copy)

    barrier = pltpu.get_barrier_semaphore()

    row_peers = [(span, (group + j) % ngroup) for j in range(ngroup)]
    column_peers = [((span + i) % nspan, group) for i in range(nspan)]
    for peer in row_peers[1:] + column_peers[1:]:
        pl.semaphore_signal(barrier, inc=1, device_id=peer, device_id_type=MESH)

    count = count_s[0]
    width = width_s[0]
    lane = iota((1, LANES), 1)

    for k in range(3):
        loads[k].wait()
    own8 = own_v[...]
    seg8 = seg_v[...]
    blk8 = blk_v[...]
    active8 = (iota((8, LANES), 0) * LANES + iota((8, LANES), 1)) < count
    sub128 = iota((LANES, LANES), 0)
    hits = [own8[c : c + 1, :] == sub128 for c in range(8)]
    upper = onehot(iota((LANES, 2 * LANES), 0) < iota((LANES, 2 * LANES), 1))
    ahead = mm(jnp.concatenate([onehot(h) for h in hits], axis=0), upper)
    carry = jnp.zeros((LANES, LANES), F32)
    ranks = []
    for c in range(8):
        part = ahead[c * LANES : (c + 1) * LANES]
        ranks.append(
            jnp.sum(jnp.where(hits[c], part[:, :LANES] + carry, F32(0.0)), axis=0, keepdims=True)
        )
        carry = carry + part[:, LANES:]
    rank8 = jnp.concatenate(ranks, axis=0)
    place8 = jnp.where(active8, own8 * CAP + rank8.astype(I32), -1)
    line8 = seg8 // LANES
    key8 = (line8 // 8) * 512 + ((seg8 % LANES) // 2) * 8 + line8 % 8
    half8 = seg8 % 2
    shift8 = jnp.where(active8, rank8.astype(I32) + group * CAP, -1)
    table = jnp.concatenate(
        [
            jnp.where(active8, place8 % 1024, -1).astype(F32),
            key8.astype(F32),
            half8.astype(F32),
            shift8.astype(F32),
            (blk8 + 1).astype(F32),
            active8.astype(F32),
            (place8 // 1024).astype(F32),
            jnp.zeros((LANES - 56, LANES), F32),
        ],
        axis=0,
    )
    columns = table.T.astype(I32)

    def column(a, c):
        return columns[:, a * 8 + c : a * 8 + c + 1]

    slots = jnp.concatenate(
        [
            jnp.where(column(3, c) == lane, column(4, c).astype(F32), F32(0.0)).astype(BF16)
            for c in range(8)
        ],
        axis=0,
    )
    spot8 = (own8 % ngroup) * nspan + own8 // ngroup
    owners = jnp.concatenate([onehot(spot8[c : c + 1, :] == sub128) for c in range(8)], axis=1)
    idx_out[...] = mm(owners, slots)

    loads[3].wait()
    for k in range(6, 9):
        loads[k].start()
    for line in range(2):
        for j in range(64):
            k = (line * 64 + j) * 8
            a = air_v[line * 8 : line * 8 + 8, j * LANES : (j + 1) * LANES]
            hi = a.astype(BF16).astype(F32)
            lo = a - hi
            z_v[k : k + 8, :LANES] = jnp.where(lane < 64, hi, pltpu.roll(lo, 64, 1))
            z_v[k : k + 8, LANES:] = jnp.where(lane < 64, pltpu.roll(hi, 64, 1), lo)
    bank[...] = z_v[...].astype(BF16)
    pl.semaphore_wait(barrier, nspan + ngroup - 2)
    for peer in row_peers[1:]:
        pl.semaphore_signal(ready, inc=1, device_id=peer, device_id_type=MESH)

    def idx_row(j):
        g = (group + j) % ngroup
        return pltpu.make_async_remote_copy(
            idx_out.at[pl.ds(pl.multiple_of(g * nspan, nspan), nspan)],
            idx_row_in.at[group],
            send_sem.at[1], recv_sem.at[1],
            device_id=(span, g), device_id_type=MESH,
        )

    for j in range(1, ngroup):
        idx_row(j).start()
    idx_row_in[group] = idx_out[pl.ds(pl.multiple_of(group * nspan, nspan), nspan), :]

    key_lane = iota((LANES, 8 * LANES), 1)
    for c in range(8):
        rows = mm(onehot(column(1, c) == key_lane), bank[...])
        rows = jnp.where(column(2, c) == 0, rows[:, :LANES], rows[:, LANES:])
        cut = slice(c * LANES, (c + 1) * LANES)
        pick[cut, :] = rows.astype(BF16)
        pick2[cut, :LANES] = jnp.where(column(6, c) == 0, rows, F32(0.0)).astype(BF16)
        pick2[cut, LANES:] = jnp.where(column(6, c) == 1, rows, F32(0.0)).astype(BF16)

    def send_rows(src, dst, k, s, skip_self):
        for n, (_, g) in enumerate(row_peers):
            copy = pltpu.make_async_remote_copy(
                src.at[s * ngroup + g], dst.at[me], send_sem.at[k], recv_sem.at[k],
                device_id=(s, g), device_id_type=MESH,
            )
            if n == 0:
                pl.when(skip_self)(copy.start)
            else:
                copy.start()

    place8m = jnp.where(active8, place8 % 1024, -1)
    pl.semaphore_wait(ready, ngroup - 1)

    def pack_and_send(i):
        u = (span + i) % 8
        slot = iota((LANES, LANES), 0) + u * LANES
        sel = jnp.concatenate([onehot(place8m[c : c + 1, :] == slot) for c in range(8)], axis=1)
        rows = mm(sel, pick2[...]).astype(BF16)
        send[pl.ds(u * ngroup, ngroup)] = rows[:, :LANES].reshape(ngroup, CAP, LANES)
        send[pl.ds((u + 8) * ngroup, ngroup)] = rows[:, LANES:].reshape(ngroup, CAP, LANES)
        for a in range(2):
            s = (span + i + 8 * a) % nspan
            send_rows(send, recv, 0, s, s != span)

    pl.loop(0, 4)(pack_and_send)
    both = pltpu.make_async_remote_copy(
        idx_row_in.at[pl.ds(0, ngroup - 1)], idx_row_in.at[pl.ds(0, ngroup - 1)],
        send_sem.at[1], recv_sem.at[1], device_id=row_peers[1], device_id_type=MESH,
    )
    both.wait_send()
    both.wait_recv()
    total = idx_row_in[0]
    for g in range(1, ngroup):
        total = total + idx_row_in[g]
    idx_mid[:, 0, :] = total

    def idx_column(i):
        s = (span + i) % nspan
        return pltpu.make_async_remote_copy(
            idx_mid.at[s], idx_in.at[span], send_sem.at[3], recv_sem.at[3],
            device_id=(s, group), device_id_type=MESH,
        )

    for i in range(1, nspan):
        idx_column(i).start()
    idx_in[span] = idx_mid[span]

    pl.loop(4, 8)(pack_and_send)

    edge_lo[0] = air_v[0:1, :]
    edge_hi[0] = air_v[15:16, :]
    field[:, LANES : LANES + 8192] = air_v[...]

    def pad_ends():
        field[:, :LANES] = jnp.broadcast_to(field[:, LANES : LANES + 1], (16, LANES))
        field[:, LANES + 8192 :] = jnp.broadcast_to(
            field[:, LANES + 8191 : LANES + 8192], (16, LANES)
        )

    pad_ends()

    def edges(step):
        east = ((span + 1) % nspan, group)
        west = ((span + nspan - 1) % nspan, group)
        return (
            pltpu.make_async_remote_copy(
                edge_hi.at[step], halo_w.at[step], edge_send.at[step, 0], edge_recv.at[step, 0],
                device_id=east, device_id_type=MESH,
            ),
            pltpu.make_async_remote_copy(
                edge_lo.at[step], halo_e.at[step], edge_send.at[step, 1], edge_recv.at[step, 1],
                device_id=west, device_id_type=MESH,
            ),
        )

    for e in edges(0):
        e.start()

    def whole(src, dst, k):
        return pltpu.make_async_remote_copy(
            src.at[pl.ds(0, ndev - 1)], dst.at[pl.ds(0, ndev - 1)], send_sem.at[k], recv_sem.at[k],
            device_id=where_is((me + 1) % ndev), device_id_type=MESH,
        )

    recv[me] = send[me]
    for c in range(8):
        slot_lane = iota((LANES, 1024), 1)
        pt_v[c * LANES : (c + 1) * LANES, :] = onehot(column(0, c) == slot_lane)

    @pl.loop(0, 8)
    def _(q):
        at = iota((LANES, LANES), 0) + q * LANES
        st_v[pl.ds(q * LANES, LANES), :] = jnp.concatenate(
            [onehot(key8[c : c + 1, :] == at) for c in range(8)], axis=1
        )

    loads[4].wait()
    nbr = (nbr_v[...] - (me - 1) * LANES).astype(F32)
    nbr8 = jnp.concatenate([nbr, nbr], axis=0)

    @pl.loop(0, 8)
    def _(q):
        tiled = jnp.concatenate([nbr8] * 16, axis=0)
        own_lane = (iota((LANES, LANES), 0) // 8 + q * 16) == iota((LANES, LANES), 1)
        link = jnp.sum(jnp.where(own_lane, tiled, F32(0.0)), axis=1, keepdims=True).astype(I32)
        near_map[pl.ds(q * LANES, LANES), :] = onehot(link == iota((LANES, 3 * LANES), 1))

    loads[6].wait()
    loads[7].wait()

    def advance(step):
        for e in edges(step):
            e.wait()
        wide = 1024
        row = iota((16, wide), 0)
        fresh = []
        for j in range(8192 // wide):
            ext = field[:, j * wide : j * wide + wide + 2 * LANES]
            t = ext[:, LANES : LANES + wide]
            north = pltpu.roll(ext, wide + 2 * LANES - 1, 1)[:, LANES : LANES + wide]
            south = pltpu.roll(ext, 1, 1)[:, LANES : LANES + wide]
            cut = slice(j * wide, (j + 1) * wide)
            east = jnp.where(row == 15, halo_e[step, :, cut], pltpu.roll(t, 15, 0))
            west = jnp.where(row == 0, halo_w[step, :, cut], pltpu.roll(t, 1, 0))
            new = (
                t
                + kap_v[:, cut] * ((east + west) + (north + south) - 4.0 * t)
                - (0.5 * vel_v[:, cut]) * (east - west)
            )
            new = jnp.where(iota((16, wide), 1) + j * wide < width, new, t)
            air_v[:, cut] = new
        field[:, LANES : LANES + 8192] = air_v[...]
        if step + 1 < STEPS:
            pad_ends()
            edge_lo[step + 1] = air_v[0:1, :]
            edge_hi[step + 1] = air_v[15:16, :]
            for e in edges(step + 1):
                e.start()

    advance(0)

    loads[5].wait()
    sub = jnp.concatenate([sub_v[...], sub_v[...]], axis=0).T
    both = pltpu.make_async_remote_copy(
        idx_mid.at[pl.ds(0, nspan - 1)], idx_in.at[pl.ds(0, nspan - 1)],
        send_sem.at[3], recv_sem.at[3], device_id=column_peers[1], device_id_type=MESH,
    )
    both.wait_send()
    both.wait_recv()
    for q in range(16):
        at = idx_in[q].astype(I32)
        t_q = jnp.where(at == iota((LANES, LANES), 0) + 1, F32(1.0), F32(0.0))
        t_v[:, q * LANES : (q + 1) * LANES] = t_q.astype(BF16)
        tt_v[q * LANES : (q + 1) * LANES, :] = t_q.T.astype(BF16)
    hits_b = mm(t_v[...], jnp.ones((2048, LANES), BF16))
    both = whole(send, recv, 0)
    both.wait_send()
    both.wait_recv()
    total = mm(t_v[...], recv[...].reshape(2048, LANES))
    total = total + pltpu.roll(total, 64, 1)
    sub = sub + UPTAKE * (total - hits_b * sub)

    def sides(step):
        nxt = where_is((me + 1) % ndev)
        prev = where_is((me + ndev - 1) % ndev)
        return (
            pltpu.make_async_remote_copy(
                beside.at[step, 1], beside.at[step, 0], side_send.at[step, 0], side_recv.at[step, 0],
                device_id=nxt, device_id_type=MESH,
            ),
            pltpu.make_async_remote_copy(
                beside.at[step, 1], beside.at[step, 2], side_send.at[step, 1], side_recv.at[step, 1],
                device_id=prev, device_id_type=MESH,
            ),
        )

    lane2 = iota((LANES, LANES), 1)
    row2 = iota((LANES, LANES), 0)
    gather_i = onehot((lane2 % 64) // 2 == row2 // 4)
    gather_i = jnp.concatenate([gather_i, gather_i], axis=0)
    per_block = onehot(iota((LANES, 8 * LANES), 1) // 8 == iota((LANES, 8 * LANES), 0))
    half_lane = (iota((8 * LANES, LANES), 0) % 8) // 4 == iota((8 * LANES, LANES), 1) // 64
    even_block = iota((8 * LANES, LANES), 0) // 8 % 2 == 0
    odd_lane = (iota((8 * LANES, LANES), 0) % 8) // 4 == iota((8 * LANES, LANES), 1) % 2
    same = iota((16, LANES), 0) % 4 == iota((16, LANES), 1) % 4

    for step in range(SSTEPS):
        beside[step, 1] = jnp.where(lane2[:64] < 64, sub[:64], sub[64:]).astype(BF16)
        for s in sides(step):
            s.start()
        advance(step + 1)
        if step == 0:
            loads[8].wait()
        for s in sides(step):
            s.wait()
        full = []
        for n in range(3):
            x = beside[step, n].astype(F32)
            y = pltpu.roll(x, 64, 1)
            full += [jnp.where(lane2[:64] < 64, x, y), jnp.where(lane2[:64] < 64, y, x)]
        near = mm(near_map[...], jnp.concatenate(full, axis=0).astype(BF16))
        near = jnp.where(half_lane, near, F32(0.0))
        near_v[:, :LANES] = jnp.where(even_block, near, F32(0.0)).astype(BF16)
        near_v[:, LANES:] = jnp.where(even_block, F32(0.0), near).astype(BF16)

        @pl.loop(0, 32, unroll=32)
        def _(p):
            quad = [c_v[pl.ds(p * 512 + b * LANES, LANES), :] for b in range(4)]
            pairs = jnp.concatenate(
                [
                    jnp.concatenate(quad[:2], axis=1),
                    jnp.concatenate(quad[2:], axis=1),
                ],
                axis=0,
            )
            res = mm_nt(near_v[pl.ds(p * 32, 32), :], pairs)
            z_v[pl.ds(p * 32, 16), :LANES] = jnp.where(same, res[:16, :LANES], F32(0.0))
            z_v[pl.ds(p * 32 + 16, 16), :LANES] = jnp.where(same, res[16:, LANES:], F32(0.0))

        hi, lo = split(z_v[:, :LANES])
        w = mm(jnp.concatenate([hi, lo], axis=1), gather_i)
        hi, lo = split(jnp.where(odd_lane, w, F32(0.0)))
        added = mm(per_block, jnp.concatenate([hi, lo], axis=1))
        sub = sub + (added[:, :LANES] + added[:, LANES:])

    hi = sub.astype(BF16).astype(F32)
    pair = jnp.where(lane2 < 64, hi, sub - hi).astype(BF16)
    @pl.loop(0, 8)
    def _(i):
        q = (span // 2 + i) % 8
        rows = mm(tt_v[pl.ds(q * 256, 256), :], pair)
        back[pl.ds(q * 16, 16)] = rows.astype(BF16).reshape(16, CAP, LANES)
        for a in range(2):
            s = q * 2 + (span + a) % 2
            send_rows(back, got, 2, s, s != span)

    got[me] = back[me]
    sub_o[...] = sub.T[:64, :]
    advance(3)
    both = whole(back, got, 2)
    both.wait_send()
    both.wait_recv()

    got2 = jnp.concatenate(
        [got[:64].reshape(1024, LANES), got[64:].reshape(1024, LANES)], axis=1
    )
    for c in range(8):
        rows = slice(c * LANES, (c + 1) * LANES)
        surf = mm(pt_v[rows, :], got2)
        surf = jnp.where(column(6, c) == 0, surf[:, :LANES], surf[:, LANES:])
        gap = surf - pick[rows, :].astype(F32)
        gap = RELEASE * (gap + pltpu.roll(gap, 64, 1))
        keep = jnp.logical_and(column(5, c) == 1, column(2, c) == lane2 // 64)
        hi, lo = split(jnp.where(keep, gap, F32(0.0)))
        bank[rows, :LANES] = hi
        bank[rows, LANES:] = lo
    z_v[...] = mm(st_v[...], bank[...])
    for line in range(2):
        for j in range(64):
            k = (line * 64 + j) * 8
            cut = slice(j * LANES, (j + 1) * LANES)
            air_o[line * 8 : line * 8 + 8, cut] = air_v[line * 8 : line * 8 + 8, cut] + (
                z_v[k : k + 8, :LANES] + z_v[k : k + 8, LANES:]
            )


def per_device(
    nspan,
    ngroup,
    air_temp,
    air_vel,
    air_kappa,
    group_width,
    sub_temp,
    sub_coupling,
    neighbors,
    iface_count,
    iface_seg,
    iface_owner,
    iface_block,
):
    cells, section = air_temp.shape[1:]
    blocks, links, _ = sub_coupling.shape
    coupling = (
        sub_coupling.reshape(blocks, links, 32, LANES)
        .transpose(0, 2, 1, 3)
        .reshape(blocks * links * 32, LANES)
    )
    ndev = nspan * ngroup
    vmem = pltpu.VMEM
    dma = pltpu.SemaphoreType.DMA
    any_space = pl.BlockSpec(memory_space=pl.ANY)
    smem = pl.BlockSpec(memory_space=pltpu.SMEM)
    in_vmem = pl.BlockSpec(memory_space=pltpu.VMEM)
    air, sub = pl.pallas_call(
        functools.partial(kernel, nspan, ngroup),
        out_shape=(
            jax.ShapeDtypeStruct((cells, section), F32),
            jax.ShapeDtypeStruct((NODES, blocks), F32),
        ),
        in_specs=[any_space] * 3 + [smem] + [any_space] * 3 + [smem] + [any_space] * 3,
        out_specs=(in_vmem, in_vmem),
        scratch_shapes=[
            vmem((cells, section), F32),
            vmem((cells, section), F32),
            vmem((cells, section), F32),
            vmem((NODES, blocks), F32),
            vmem(coupling.shape, BF16),
            vmem((links, blocks), I32),
            vmem((8, LANES), I32),
            vmem((8, LANES), I32),
            vmem((8, LANES), I32),
            vmem((cells, section + 2 * LANES), F32),
            vmem((8 * LANES, 2 * LANES), BF16),
            vmem((8 * LANES, LANES), BF16),
            vmem((8 * LANES, 2 * LANES), BF16),
            vmem((ndev, CAP, LANES), BF16),
            vmem((ndev, CAP, LANES), BF16),
            vmem((ndev, CAP, LANES), BF16),
            vmem((ndev, CAP, LANES), BF16),
            vmem((ndev, LANES), F32),
            vmem((ngroup, nspan, LANES), F32),
            vmem((nspan, 1, LANES), F32),
            vmem((nspan, 1, LANES), F32),
            vmem((LANES, ndev * CAP), BF16),
            vmem((ndev * CAP, LANES), BF16),
            vmem((8 * LANES, ndev * CAP // 2), BF16),
            vmem((8 * LANES, 8 * LANES), BF16),
            vmem((8 * LANES, 3 * LANES), BF16),
            vmem((8 * LANES, 2 * LANES), BF16),
            vmem((8 * LANES, 2 * LANES), F32),
            vmem((SSTEPS, 3, LANES // 2, LANES), BF16),
            vmem((STEPS, 1, section), F32),
            vmem((STEPS, 1, section), F32),
            vmem((STEPS, 1, section), F32),
            vmem((STEPS, 1, section), F32),
            dma((9,)),
            dma((4,)),
            dma((4,)),
            dma((STEPS, 2)),
            dma((STEPS, 2)),
            dma((SSTEPS, 2)),
            dma((SSTEPS, 2)),
            pltpu.SemaphoreType.REGULAR,
        ],
        compiler_params=pltpu.CompilerParams(
            collective_id=0, has_side_effects=True, vmem_limit_bytes=28 << 20
        ),
    )(
        pltpu.with_memory_space_constraint(air_temp.reshape(cells, section), pltpu.HBM),
        pltpu.with_memory_space_constraint(air_vel.reshape(cells, section), pltpu.HBM),
        pltpu.with_memory_space_constraint(air_kappa.reshape(cells, section), pltpu.HBM),
        group_width,
        pltpu.with_memory_space_constraint(sub_temp.T, pltpu.HBM),
        pltpu.with_memory_space_constraint(coupling, pltpu.HBM),
        pltpu.with_memory_space_constraint(neighbors.T, pltpu.HBM),
        iface_count,
        pltpu.with_memory_space_constraint(iface_seg.reshape(8, LANES), pltpu.HBM),
        pltpu.with_memory_space_constraint(iface_owner.reshape(8, LANES), pltpu.HBM),
        pltpu.with_memory_space_constraint(iface_block.reshape(8, LANES), pltpu.HBM),
    )
    return air.reshape(1, cells, section), sub.T


def solution(mesh):
    placed = (
        P("group", "span", None),
        P("group", "span", None),
        P("group", "span", None),
        P("group"),
        P(("span", "group"), None),
        P(("span", "group"), None, None),
        P(("span", "group"), None),
        P(("span", "group")),
        P(("span", "group")),
        P(("span", "group"), None),
        P(("span", "group")),
    )
    return jax.shard_map(
        functools.partial(per_device, mesh.shape["span"], mesh.shape["group"]),
        mesh=mesh,
        in_specs=placed,
        out_specs=(P("group", "span", None), P(("span", "group"), None)),
        check_vma=False,
    )
```
